32 devices in a mesh: dom: 16 (over z, y, x), feat: 2 (over core).
Axes of the slice: x: 2, y: 2, z: 4, core: 2. Of those that a mesh axis runs over, the one named last changes fastest.
Arguments:
- features: bfloat16 [16384, 512], P('dom', 'feat'), may hold values from -6 to 6
- grad_out: bfloat16 [16384, 512], P('dom', 'feat'), may hold values from -6 to 6
- pre_act: bfloat16 [16384, 512], P('dom', 'feat'), may hold values from -6 to 6
- neigh_mean: bfloat16 [16384, 512], P('dom', 'feat'), may hold values from -6 to 6
- w_self: bfloat16 [512, 512], P('feat'), may hold values from -0.25 to 0.25
- w_neigh: bfloat16 [512, 512], P('feat'), may hold values from -0.25 to 0.25
- edge_from: int32 [131072], P('dom'), may hold values from 0 to 1535
- edge_to: int32 [131072], P('dom'), may hold values from 0 to 1535
- edge_count: int32 [16], P('dom'), may hold values from 2048 to 8192, as said below
- mirror_master: int32 [8192], P('dom'), may hold values from 0 to 63
- degrees: int32 [16384], P('dom'), may hold values from 1 to 16
Outputs:
- input_grad: bfloat16 [16384, 512], P('dom', 'feat')
- self_weight_grad: float32 [512, 512], P('feat')
- neigh_weight_grad: float32 [512, 512], P('feat')
The draws below stay inside these ranges and needn't reach their ends.
Inputs may be any that keep to these rules, and one draw needn't show every extreme that they name: `edge_count`: equals 8192 in at least one partition.
All inputs are finite; a program needn't handle non-finite values.
Results may differ from the reference program's by a relative error of at most 0.0044.
Values may be sent and summed in bfloat16 or wider, within the bound.
A program may use at most 64 MiB of HBM per device.

```python
import math
import jax
import jax.numpy as jnp
import numpy as np
from jax import lax

D = 512
M_DEV = 1024
SLOT = 32
HUB = 64
E_DEV = 8192
LOCAL = 1536
NV = 16384
NE = 131072
N_DOM = 16


def draw_edge_count(key, part):
    counts = jax.random.randint(key, (N_DOM,), E_DEV // 4, E_DEV + 1)
    chosen = jax.random.randint(jax.random.fold_in(key, 7), (), 0, N_DOM)
    return counts.at[chosen].set(E_DEV).astype(jnp.int32)


def place_ends(drawn, key, smallest, top_value):
    spot = [jax.random.randint(jax.random.fold_in(key, axis), (), 0, length) for axis, length in enumerate(drawn.shape)]
    main_axis = drawn.shape.index(max(drawn.shape))
    beside = spot[:main_axis] + [(spot[main_axis] + 1) % drawn.shape[main_axis]] + spot[main_axis + 1:]
    return drawn.at[tuple(spot)].set(smallest).at[tuple(beside)].set(top_value)


def shard_levels(stream_key, extent, shards, smallest, largest):
    level = 1.0
    for axis_at, blocks in shards:
        draws = jax.random.uniform(jax.random.fold_in(jax.random.fold_in(stream_key, 6), axis_at), (blocks,), jnp.float32, smallest / len(shards), largest / len(shards))
        level = level * jnp.repeat(jnp.exp(draws), extent[axis_at] // blocks).reshape((-1,) + (1,) * (len(extent) - 1 - axis_at))
    return level


def rank_table(count, skew):
    loads = [(1 << 20) // math.isqrt(grade ** skew) + 1 for grade in range(1, count + 1)]
    deviation = 1 + sum(loads) // (1 << 30)
    return np.cumsum(np.array([max(1, weight // deviation) for weight in loads]))


def ranked(own_key, extent, amount, lean):
    table = rank_table(amount, lean)
    lot = jax.random.randint(jax.random.fold_in(own_key, 1), extent, 0, int(table[amount - 1]))
    standing = jnp.searchsorted(jnp.asarray(table, jnp.int32), lot, side="right")
    return jax.random.permutation(jax.random.fold_in(own_key, 2), amount)[standing].astype(jnp.int32)


def scatter_about(key, extent, deviation, limit, shards=(), kind=jnp.bfloat16):
    entries = deviation * jax.random.normal(key, extent, jnp.float32)
    if shards:
        entries = entries * shard_levels(key, extent, shards, -0.22, 0.18)
    return jnp.clip(entries, -limit, limit).astype(kind)


def setup_inputs(seed: int = 0) -> dict:
    keys = jax.random.split(jax.random.key(seed), 12)
    return {
        "features": scatter_about(keys[0], (NV, D), 1.0, 6.0, ((0, 16), (1, 2))),
        "grad_out": scatter_about(keys[1], (NV, D), 1.0, 6.0, ((0, 16), (1, 2))),
        "pre_act": scatter_about(keys[2], (NV, D), 1.0, 6.0, ((0, 16), (1, 2))),
        "neigh_mean": scatter_about(keys[3], (NV, D), 1.0, 6.0, ((0, 16), (1, 2))),
        "w_self": scatter_about(keys[4], (D, D), D ** -0.5, 0.25, ((0, 2),)),
        "w_neigh": scatter_about(keys[5], (D, D), D ** -0.5, 0.25, ((0, 2),)),
        "edge_from": place_ends(jax.random.randint(keys[6], (NE,), 0, LOCAL), jax.random.fold_in(keys[6], 1), 0, LOCAL - 1).astype(jnp.int32),
        "edge_to": place_ends(ranked(keys[7], (NE,), LOCAL, 2), jax.random.fold_in(keys[7], 3), 0, LOCAL - 1).astype(jnp.int32),
        "edge_count": draw_edge_count(jax.random.fold_in(keys[11], 71), 0),
        "mirror_master": place_ends(jax.random.randint(keys[9], (N_DOM * N_DOM * SLOT,), 0, HUB), jax.random.fold_in(keys[9], 1), 0, HUB - 1).astype(jnp.int32),
        "degrees": place_ends(jax.random.randint(keys[10], (NV,), 1, 17), jax.random.fold_in(keys[10], 1), 1, 16).astype(jnp.int32),
    }


def reference(features, grad_out, pre_act, neigh_mean, w_self, w_neigh, edge_from, edge_to, edge_count, mirror_master, degrees):
    grad_pre = (grad_out.astype(jnp.float32) * (pre_act > 0).astype(jnp.float32)).astype(jnp.bfloat16)
    self_weight_grad = jnp.dot(features.T, grad_pre, preferred_element_type=jnp.float32)
    neigh_weight_grad = jnp.dot(neigh_mean.T, grad_pre, preferred_element_type=jnp.float32)
    self_part = jnp.dot(grad_pre, w_self.T, preferred_element_type=jnp.float32)
    neigh_part = jnp.dot(grad_pre, w_neigh.T, preferred_element_type=jnp.float32)
    scaled = (neigh_part / degrees[:, None].astype(jnp.float32)).astype(jnp.bfloat16)
    mirror_count = N_DOM * SLOT
    local_rows = M_DEV + mirror_count
    owners = jnp.arange(mirror_count, dtype=jnp.int32) // SLOT

    def partition_step(index, totals):
        index = jnp.asarray(index).astype(jnp.int32)
        row_base = (index * M_DEV).astype(jnp.int32)
        masters = lax.dynamic_slice_in_dim(scaled, row_base, M_DEV, 0)
        targets = lax.dynamic_slice_in_dim(mirror_master, (index * mirror_count).astype(jnp.int32), mirror_count, 0)
        global_rows = (owners * M_DEV + targets).astype(jnp.int32)
        tables = jnp.concatenate([masters, scaled[global_rows]], axis=0)
        edge_base = (index * E_DEV).astype(jnp.int32)
        sources = lax.dynamic_slice_in_dim(edge_from, edge_base, E_DEV, 0)
        sinks = lax.dynamic_slice_in_dim(edge_to, edge_base, E_DEV, 0)
        is_live = jnp.arange(E_DEV, dtype=jnp.int32) < edge_count[index]
        contrib = jnp.where(is_live[:, None], tables[sinks].astype(jnp.float32), jnp.float32(0.0))
        summed = jax.ops.segment_sum(contrib, sources, num_segments=local_rows)
        mirror_grad = lax.optimization_barrier(summed[M_DEV:].astype(jnp.bfloat16)).astype(jnp.float32)
        current = lax.dynamic_slice_in_dim(totals, row_base, M_DEV, 0)
        totals = lax.dynamic_update_slice_in_dim(totals, current + summed[:M_DEV], row_base, 0)
        return totals.at[global_rows].add(mirror_grad)

    edge_grad = lax.fori_loop(0, N_DOM, partition_step, jnp.zeros((M_DEV * N_DOM, D), jnp.float32))
    input_grad = (self_part + edge_grad).astype(jnp.bfloat16)
    return input_grad, self_weight_grad, neigh_weight_grad
```

```python
import functools

import jax
import jax.numpy as jnp
from jax import lax
from jax.experimental import pallas as pl
from jax.experimental.pallas import tpu as pltpu
from jax.sharding import PartitionSpec as P

LANES = 128
HUBS = 64
MESH = pl.DeviceIdType.MESH
F32, BF16, F8 = jnp.float32, jnp.bfloat16, jnp.float8_e4m3fn


def dot(a, b, over):
    return lax.dot_general(a, b, ((over[:1], over[1:]), ((), ())), preferred_element_type=F32)


def columns_of(row):
    return jnp.transpose(jnp.broadcast_to(row, (LANES, LANES)))


def pick_rows(sinks, first, count):
    one, zero = jnp.ones((), BF16), jnp.zeros((), BF16)
    lane = lax.broadcasted_iota(jnp.int32, (LANES, LANES), 1)
    tiles = []
    for g in range(sinks.shape[0]):
        column = columns_of(sinks[g : g + 1, :])
        tiles.append(
            jnp.concatenate(
                [jnp.where(column == lane + (first + j), one, zero) for j in range(0, count, LANES)],
                axis=1,
            )
        )
    return jnp.concatenate(tiles, axis=0)


def put_rows(sources, first, count):
    one, zero = jnp.ones((), BF16), jnp.zeros((), BF16)
    row = lax.broadcasted_iota(jnp.int32, (count, LANES), 0) + first
    return jnp.concatenate(
        [jnp.where(row == sources[g : g + 1, :], one, zero) for g in range(sources.shape[0])],
        axis=1,
    )


def layer_kernel(
    parts,
    block,
    limit_ref,
    grad_ref,
    pre_ref,
    features_hbm,
    mean_hbm,
    w_self_hbm,
    w_neigh_hbm,
    source_ref,
    sink_ref,
    wanted_ref,
    degree_ref,
    out_ref,
    weights_ref,
    features_ref,
    mean_ref,
    w_self_ref,
    w_neigh_ref,
    cols,
    live,
    table,
    asked,
    replies,
    mirrors,
    picked,
    master_sum,
    mirror_sum,
    returns,
    returned,
    hits,
    partial,
    arrived,
    column_sum,
    column_arrived,
    column_total,
    full,
    load_sems,
    feat_sems,
    send_sems,
    recv_sems,
):
    me, half = lax.axis_index("dom"), lax.axis_index("feat")
    partner = 1 - half
    masters, width = grad_ref.shape
    slots = wanted_ref.shape[2]
    low, low_rows = partial.shape[0], partial.shape[1]
    owners, chunk = column_sum.shape[0], column_sum.shape[1]
    high = parts // low
    at_high, at_low = me // low, lax.rem(me, low)
    groups = block // LANES
    blocks = sink_ref.shape[0] // groups

    def peer(k):
        return lax.rem(me + k, parts)

    def giver(k):
        return lax.rem(me + (parts - k), parts)

    def rows_of(q):
        return pl.ds(pl.multiple_of(q * slots, slots), slots)

    def copy(stage, k, src, dst, device=None):
        return pltpu.make_async_remote_copy(
            src_ref=src,
            dst_ref=dst,
            send_sem=send_sems.at[stage, k],
            recv_sem=recv_sems.at[stage, k],
            device_id={"dom": peer(k) if device is None else device},
            device_id_type=MESH,
        )

    def each_peer(act, count=parts):
        lax.fori_loop(1, count, lambda k, c: (act(k), c)[1], 0)

    loads = [
        pltpu.make_async_copy(src, dst, load_sems.at[i])
        for i, (src, dst) in enumerate(
            (
                (w_neigh_hbm, w_neigh_ref),
                (features_hbm, features_ref),
                (mean_hbm, mean_ref),
                (w_self_hbm, w_self_ref),
            )
        )
    ]

    barrier = pltpu.get_barrier_semaphore()
    pl.semaphore_signal(barrier, inc=1, device_id={"feat": partner}, device_id_type=MESH)
    each_peer(
        lambda k: pl.semaphore_signal(
            barrier, inc=1, device_id={"dom": peer(k)}, device_id_type=MESH
        )
    )
    for load in loads:
        load.start()
    keep = (pre_ref[...] > 0).astype(F32)
    cols[half] = (grad_ref[...].astype(F32) * keep).astype(BF16)
    place = (
        lax.broadcasted_iota(jnp.int32, source_ref.shape, 0) * LANES
        + lax.broadcasted_iota(jnp.int32, source_ref.shape, 1)
    )
    live[...] = jnp.where(place < limit_ref[0], source_ref[...], -1)
    asked[me] = wanted_ref[me]
    pl.semaphore_wait(barrier, parts)

    exchange = pltpu.make_async_remote_copy(
        src_ref=cols.at[half],
        dst_ref=cols.at[half],
        send_sem=feat_sems.at[0],
        recv_sem=feat_sems.at[1],
        device_id={"feat": partner},
        device_id_type=MESH,
    )
    exchange.start()

    def request(k):
        return copy(0, k, wanted_ref.at[peer(k)], asked.at[me])

    each_peer(lambda k: request(k).start())
    def half_at(h):
        return pl.ds(pl.multiple_of(h * width, width), width)

    loads[0].wait()
    own = dot(cols[half], w_neigh_ref[:, half_at(half)], (1, 1))
    pltpu.make_async_remote_copy(
        src_ref=cols.at[half],
        dst_ref=cols.at[partner],
        send_sem=feat_sems.at[0],
        recv_sem=feat_sems.at[1],
        device_id={"feat": partner},
        device_id_type=MESH,
    ).wait_recv()

    both = jnp.concatenate([cols[0], cols[1]], axis=1)
    per_weight = low // 2
    for i, operand in enumerate((features_ref, mean_ref)):
        loads[1 + i].wait()
        part = dot(operand[...], both, (0, 0)).astype(BF16)
        for c in range(per_weight):
            partial[i * per_weight + c] = part[c * low_rows : (c + 1) * low_rows, :]

    def low_peer(k):
        return lax.rem(at_low + k, low)

    def low_giver(k):
        return lax.rem(at_low + (low - k), low)

    def high_peer(k):
        return lax.rem(at_high + k, high)

    def high_giver(k):
        return lax.rem(at_high + (high - k), high)

    def to_low(stage, k, src, dst):
        return copy(stage, k, src, dst, at_high * low + low_peer(k))

    def to_high(stage, k, src, dst):
        return copy(stage, k, src, dst, high_peer(k) * low + at_low)

    def guarded(act, owner):
        if owners == high:
            return act
        return lambda k: pl.when(owner(k) < owners)(lambda: act(k))

    def if_owner(act):
        if owners == high:
            act()
        else:
            pl.when(at_high < owners)(act)

    def scatter(k):
        return to_low(2, k, partial.at[low_peer(k)], arrived.at[at_low])

    each_peer(lambda k: scatter(k).start(), low)
    neigh = own + dot(cols[partner], w_neigh_ref[:, half_at(partner)], (1, 1))
    for g in range(masters // LANES):
        at = slice(g * LANES, (g + 1) * LANES)
        degree = columns_of(degree_ref[g : g + 1, :]).astype(F32)
        degree = jnp.concatenate([degree] * (width // LANES), axis=1)
        table[at, :] = (neigh[at, :] / degree).astype(BF16)

    each_peer(lambda k: copy(0, k, wanted_ref.at[peer(k)], asked.at[giver(k)]).wait_recv())

    batch = 8 if parts % 8 == 0 else 1
    hub = lax.broadcasted_iota(jnp.int32, (HUBS, slots), 0)

    def batch_at(i):
        return pl.ds(pl.multiple_of(i * batch * slots, batch * slots), batch * slots)

    def answer(i, c):
        hit = jnp.concatenate(
            [
                jnp.where(hub == asked[i * batch + j], jnp.ones((), BF16), jnp.zeros((), BF16))
                for j in range(batch)
            ],
            axis=1,
        )
        hits[i] = hit
        replies[batch_at(i), :] = dot(hit, table[:HUBS, :], (0, 0)).astype(BF16)
        return c

    lax.fori_loop(0, parts // batch, answer, 0)
    mirrors[rows_of(me), :] = replies[rows_of(me), :]

    def reply(k):
        return copy(1, k, replies.at[rows_of(peer(k)), :], mirrors.at[rows_of(me), :])

    each_peer(lambda k: reply(k).start())

    def block_at(b):
        return pl.ds(pl.multiple_of(b * groups, groups), groups)

    def edges_at(b):
        return pl.ds(pl.multiple_of(b * block, block), block)

    def from_masters(b, c):
        pick = pick_rows(sink_ref[block_at(b), :], 0, masters)
        picked[edges_at(b), :] = dot(pick, table[...], (1, 0)).astype(BF16)
        return c

    lax.fori_loop(0, blocks, from_masters, 0)

    each_peer(
        lambda k: to_low(2, k, partial.at[low_peer(k)], arrived.at[low_giver(k)]).wait_recv(), low
    )
    total = lax.fori_loop(
        1,
        low,
        lambda k, t: t + arrived[low_giver(k)].astype(F32),
        partial[at_low].astype(F32),
    ).astype(BF16)
    for c in range(owners):
        column_sum[c] = total[c * chunk : (c + 1) * chunk, :]

    def column_place():
        return lax.rem(at_high, owners)

    def scatter_high(k):
        return to_high(
            4, k, column_sum.at[lax.rem(high_peer(k), owners)], column_arrived.at[at_high]
        )

    each_peer(guarded(lambda k: scatter_high(k).start(), high_peer), high)

    each_peer(
        lambda k: copy(
            1, k, replies.at[rows_of(peer(k)), :], mirrors.at[rows_of(giver(k)), :]
        ).wait_recv()
    )
    mirror_sum[...] = jnp.zeros_like(mirror_sum)
    mirror_count = mirrors.shape[0]

    def from_mirrors(b, c):
        pick = pick_rows(sink_ref[block_at(b), :], masters, mirror_count)
        more = dot(pick, mirrors[...], (1, 0)).astype(BF16)
        row = picked[edges_at(b), :] + more
        picked[edges_at(b), :] = row
        return c

    lax.fori_loop(0, blocks, from_mirrors, 0)

    def column_spread(k):
        return to_high(5, k, column_total.at[column_place()], column_total.at[column_place()])

    def reduce_column():
        each_peer(
            lambda k: to_high(
                4,
                k,
                column_sum.at[lax.rem(high_peer(k), owners)],
                column_arrived.at[high_giver(k)],
            ).wait_recv(),
            high,
        )
        column_total[column_place()] = lax.fori_loop(
            1,
            high,
            lambda k, t: t + column_arrived[high_giver(k)].astype(F32),
            column_sum[column_place()].astype(F32),
        ).astype(BF16)
        each_peer(lambda k: column_spread(k).start(), high)

    if_owner(reduce_column)

    def to_mirrors(b, c):
        put = put_rows(live[block_at(b), :], masters, mirror_count)
        mirror_sum[...] += dot(put, picked[edges_at(b), :], (1, 0))
        return c

    lax.fori_loop(0, blocks, to_mirrors, 0)
    returns[...] = mirror_sum[...].astype(BF16)
    returned[rows_of(me), :] = returns[rows_of(me), :]

    def give_back(k):
        return copy(3, k, returns.at[rows_of(peer(k)), :], returned.at[rows_of(me), :])

    each_peer(lambda k: give_back(k).start())

    each_peer(
        guarded(
            lambda k: to_high(
                5,
                k,
                column_total.at[column_place()],
                column_total.at[lax.rem(high_giver(k), owners)],
            ).wait_recv(),
            high_giver,
        ),
        high,
    )
    full[at_low] = column_total[...]

    def spread(k):
        return to_low(6, k, column_total, full.at[at_low])

    each_peer(lambda k: spread(k).start(), low)

    loads[3].wait()
    master_sum[...] = dot(cols[0], w_self_ref[:, :width], (1, 1)) + dot(
        cols[1], w_self_ref[:, width:], (1, 1)
    )

    def to_masters(b, c):
        put = put_rows(live[block_at(b), :], 0, masters)
        master_sum[...] += dot(put, picked[edges_at(b), :], (1, 0))
        return c

    lax.fori_loop(0, blocks, to_masters, 0)

    each_peer(
        lambda k: copy(
            3, k, returns.at[rows_of(peer(k)), :], returned.at[rows_of(giver(k)), :]
        ).wait_recv()
    )
    hub_sum = lax.fori_loop(
        0,
        parts // batch,
        lambda i, t: t + dot(hits[i], returned[batch_at(i), :], (1, 0)),
        master_sum[:HUBS, :],
    )
    out_ref[:HUBS, :] = hub_sum.astype(BF16)
    out_ref[HUBS:, :] = master_sum[HUBS:, :].astype(BF16)

    each_peer(lambda k: to_low(6, k, column_total, full.at[low_giver(k)]).wait_recv(), low)
    weights_ref[...] = full[...]

    exchange.wait_send()
    each_peer(lambda k: request(k).wait_send())
    each_peer(lambda k: reply(k).wait_send())
    each_peer(lambda k: give_back(k).wait_send())
    each_peer(lambda k: scatter(k).wait_send(), low)
    each_peer(guarded(lambda k: scatter_high(k).wait_send(), high_peer), high)
    if_owner(lambda: each_peer(lambda k: column_spread(k).wait_send(), high))
    each_peer(lambda k: spread(k).wait_send(), low)


def ones_at(index, count, first):
    one, zero = jnp.ones((), BF16), jnp.zeros((), BF16)
    row = (lax.broadcasted_iota(jnp.int32, (count, LANES), 0) + first).astype(jnp.int16)
    index = index.astype(jnp.int16)
    return jnp.concatenate(
        [
            jnp.where(row == index[g : g + 1, :], one, zero).astype(F8)
            for g in range(index.shape[0])
        ],
        axis=1,
    )


def count_kernel(
    parts,
    low,
    block,
    limit_ref,
    grad_hbm,
    pre_hbm,
    features_hbm,
    mean_hbm,
    w_self_hbm,
    w_neigh_hbm,
    source_hbm,
    sink_hbm,
    wanted_hbm,
    degree_hbm,
    out_ref,
    self_ref,
    neigh_ref,
    grad_ref,
    pre_ref,
    features_ref,
    mean_ref,
    w_self_ref,
    w_neigh_ref,
    source_ref,
    sink_ref,
    asking,
    degree_ref,
    wanted,
    cols,
    table,
    asked,
    replies,
    mirrors,
    master_sum,
    returns,
    returned,
    hits,
    sinks,
    count_sum,
    counts,
    partial,
    arrived,
    column_sum,
    column_arrived,
    column_total,
    full,
    load_sems,
    feat_send,
    feat_recv,
    send_sems,
    recv_sems,
):
    me, half = lax.axis_index("dom"), lax.axis_index("feat")
    partner = 1 - half
    masters, width = grad_ref.shape
    slots = wanted.shape[2]
    mirror_count = mirrors.shape[0]
    rows = masters + mirror_count
    low_rows = partial.shape[2]
    high, chunk = column_sum.shape[1], column_sum.shape[2]
    at_high, at_low = me // low, lax.rem(me, low)
    groups = block // LANES
    blocks = sink_ref.shape[0] // groups
    step = mirror_count // 2
    column_halves = (half, partner)

    def peer(k):
        return lax.rem(me + k, parts)

    def giver(k):
        return lax.rem(me + (parts - k), parts)

    def rows_of(q):
        return pl.ds(pl.multiple_of(q * slots, slots), slots)

    def half_at(h):
        return pl.ds(pl.multiple_of(h * width, width), width)

    def copy(stage, k, src, dst, device=None):
        return pltpu.make_async_remote_copy(
            src_ref=src,
            dst_ref=dst,
            send_sem=send_sems.at[stage, k],
            recv_sem=recv_sems.at[stage, k],
            device_id={"dom": peer(k) if device is None else device},
            device_id_type=MESH,
        )

    def across(i, src, dst):
        return pltpu.make_async_remote_copy(
            src_ref=src,
            dst_ref=dst,
            send_sem=feat_send.at[i],
            recv_sem=feat_recv.at[i],
            device_id={"feat": partner},
            device_id_type=MESH,
        )

    def each_peer(act, count=parts):
        lax.fori_loop(1, count, lambda k, c: (act(k), c)[1], 0)

    loads = [
        pltpu.make_async_copy(src, dst, load_sems.at[i])
        for i, (src, dst) in enumerate(
            (
                (grad_hbm, grad_ref),
                (pre_hbm, pre_ref),
                (features_hbm, features_ref),
                (mean_hbm, mean_ref),
                (wanted_hbm, asking),
                (w_neigh_hbm, w_neigh_ref),
                (degree_hbm, degree_ref),
                (source_hbm, source_ref),
                (sink_hbm, sink_ref),
                (w_self_hbm, w_self_ref),
            )
        )
    ]

    barrier = pltpu.get_barrier_semaphore()
    pl.semaphore_signal(barrier, inc=1, device_id={"feat": partner}, device_id_type=MESH)
    each_peer(
        lambda k: pl.semaphore_signal(
            barrier, inc=1, device_id={"dom": peer(k)}, device_id_type=MESH
        )
    )
    for load in loads:
        load.start()
    loads[0].wait()
    loads[1].wait()
    keep = (pre_ref[...] > 0).astype(F32)
    cols[half] = (grad_ref[...].astype(F32) * keep).astype(BF16)

    per_weight = low // 2

    def weigh(h):
        for i, operand in enumerate((features_ref, mean_ref)):
            part = dot(operand[...], cols[h], (0, 0)).astype(BF16)
            for c in range(per_weight):
                partial[h, i * per_weight + c] = part[c * low_rows : (c + 1) * low_rows, :]

    def low_peer(k):
        return lax.rem(at_low + k, low)

    def low_giver(k):
        return lax.rem(at_low + (low - k), low)

    def high_peer(k):
        return lax.rem(at_high + k, high)

    def high_giver(k):
        return lax.rem(at_high + (high - k), high)

    def to_low(stage, k, src, dst):
        return copy(stage, k, src, dst, at_high * low + low_peer(k))

    def to_high(stage, k, src, dst):
        return copy(stage, k, src, dst, high_peer(k) * low + at_low)

    def scatter(i, k):
        h = column_halves[i]
        return to_low(3 + i, k, partial.at[h, low_peer(k)], arrived.at[h, at_low])

    def scatter_high(i, k):
        h = column_halves[i]
        return to_high(5 + i, k, column_sum.at[h, high_peer(k)], column_arrived.at[h, at_high])

    def spread_high(i, k):
        h = column_halves[i]
        return to_high(7 + i, k, column_total.at[h, at_high], column_total.at[h, at_high])

    def spread(i, k):
        h = column_halves[i]
        return to_low(9 + i, k, column_total.at[h], full.at[h, at_low])

    def add_low(i):
        h = column_halves[i]
        each_peer(
            lambda k: to_low(
                3 + i, k, partial.at[h, low_peer(k)], arrived.at[h, low_giver(k)]
            ).wait_recv(),
            low,
        )
        total = partial[h, at_low].astype(F32)
        for k in range(1, low):
            total = total + arrived[h, low_giver(k)].astype(F32)
        total = total.astype(BF16)
        for c in range(high):
            column_sum[h, c] = total[c * chunk : (c + 1) * chunk, :]
        each_peer(lambda k: scatter_high(i, k).start(), high)

    def add_high(i):
        h = column_halves[i]
        each_peer(
            lambda k: to_high(
                5 + i, k, column_sum.at[h, high_peer(k)], column_arrived.at[h, high_giver(k)]
            ).wait_recv(),
            high,
        )
        total = column_sum[h, at_high].astype(F32)
        for k in range(1, high):
            total = total + column_arrived[h, high_giver(k)].astype(F32)
        column_total[h, at_high] = total.astype(BF16)
        each_peer(lambda k: spread_high(i, k).start(), high)

    def pass_on(i):
        h = column_halves[i]
        each_peer(
            lambda k: to_high(
                7 + i, k, column_total.at[h, at_high], column_total.at[h, high_giver(k)]
            ).wait_recv(),
            high,
        )
        each_peer(lambda k: spread(i, k).start(), low)
        full[h, at_low] = column_total[h]

    def finish(i):
        h = column_halves[i]
        each_peer(
            lambda k: to_low(9 + i, k, column_total.at[h], full.at[h, low_giver(k)]).wait_recv(),
            low,
        )
        for w, ref in enumerate((self_ref, neigh_ref)):
            for c in range(per_weight):
                for z in range(high):
                    at = c * low_rows + z * chunk
                    ref[at : at + chunk, half_at(h)] = full[h, w * per_weight + c, z].astype(F32)

    loads[2].wait()
    loads[3].wait()
    weigh(half)
    loads[4].wait()
    per_row = LANES // slots
    for p in range(parts):
        at = (p % per_row) * slots
        wanted[p] = asking[p // per_row : p // per_row + 1, at : at + slots]
    asked[me] = wanted[me]
    pl.semaphore_wait(barrier, parts)

    exchange = across(0, cols.at[half], cols.at[half])
    exchange.start()

    def request(k):
        return copy(0, k, wanted.at[peer(k)], asked.at[me])

    each_peer(lambda k: request(k).start())
    each_peer(lambda k: scatter(0, k).start(), low)
    loads[5].wait()
    loads[6].wait()
    own = dot(cols[half], w_neigh_ref[:, half_at(half)], (1, 1))
    loads[7].wait()
    place = (
        lax.broadcasted_iota(jnp.int32, source_ref.shape, 0) * LANES
        + lax.broadcasted_iota(jnp.int32, source_ref.shape, 1)
    )
    source_ref[...] = jnp.where(place < limit_ref[0], source_ref[...], -1)
    across(0, cols.at[half], cols.at[partner]).wait_recv()
    weigh(partner)
    each_peer(lambda k: scatter(1, k).start(), low)

    neigh = own + dot(cols[partner], w_neigh_ref[:, half_at(partner)], (1, 1))
    for g in range(masters // LANES):
        at = slice(g * LANES, (g + 1) * LANES)
        degree = columns_of(degree_ref[g : g + 1, :]).astype(F32)
        degree = jnp.concatenate([degree] * (width // LANES), axis=1)
        table[at, :] = (neigh[at, :] / degree).astype(BF16)

    each_peer(lambda k: copy(0, k, wanted.at[peer(k)], asked.at[giver(k)]).wait_recv())

    batch = 8 if parts % 8 == 0 else 1
    hub = lax.broadcasted_iota(jnp.int32, (HUBS, slots), 0)

    def batch_at(i):
        return pl.ds(pl.multiple_of(i * batch * slots, batch * slots), batch * slots)

    def answer(i, c):
        hit = jnp.concatenate(
            [
                jnp.where(hub == asked[i * batch + j], jnp.ones((), BF16), jnp.zeros((), BF16))
                for j in range(batch)
            ],
            axis=1,
        )
        hits[i] = hit
        replies[batch_at(i), :] = dot(hit, table[:HUBS, :], (0, 0)).astype(BF16)
        return c

    lax.fori_loop(0, parts // batch, answer, 0)

    def reply(k):
        return copy(1, k, replies.at[rows_of(peer(k)), :], mirrors.at[rows_of(me), :])

    each_peer(lambda k: reply(k).start())
    mirrors[rows_of(me), :] = replies[rows_of(me), :]

    def count_at(r, h):
        first = masters + h * step if r == 0 else h * (masters // 2) + (r - 1) * step
        return pl.ds(pl.multiple_of(first, step), step)

    def block_at(b):
        return pl.ds(b * groups, groups)

    def count(r):
        def term(b):
            if r == 0:
                sinks[b] = ones_at(sink_ref[block_at(b), :], rows, 0)
            first = masters + half * step if r == 0 else half * (masters // 2) + (r - 1) * step
            source = ones_at(source_ref[block_at(b), :], step, first)
            return dot(source, sinks[b], (1, 1))

        count_sum[...] = term(0)
        for b in range(1, blocks - 1):
            count_sum[...] += term(b)
        counts[count_at(r, half), :] = (count_sum[...] + term(blocks - 1)).astype(BF16)
        across(1 + r, counts.at[count_at(r, half), :], counts.at[count_at(r, half), :]).start()

    def count_arrives(r):
        across(1 + r, counts.at[count_at(r, half), :], counts.at[count_at(r, partner), :]).wait_recv()

    def give_back(k):
        return copy(2, k, returns.at[rows_of(peer(k)), :], returned.at[rows_of(me), :])

    loads[8].wait()
    count(0)
    add_low(0)
    add_low(1)
    count(1)
    add_high(0)
    add_high(1)
    count_arrives(0)
    own_part = dot(counts[masters:, :masters], table[...], (1, 0))
    each_peer(
        lambda k: copy(
            1, k, replies.at[rows_of(peer(k)), :], mirrors.at[rows_of(giver(k)), :]
        ).wait_recv()
    )
    mirror_sum = own_part + dot(counts[masters:, masters:], mirrors[...], (1, 0))
    returns[...] = mirror_sum.astype(BF16)
    each_peer(lambda k: give_back(k).start())
    returned[rows_of(me), :] = returns[rows_of(me), :]
    pass_on(0)
    last = masters // mirror_count
    for r in range(2, last):
        count(r)
    count(last)
    pass_on(1)
    loads[9].wait()
    master_sum[...] = (
        dot(cols[0], w_self_ref[:, :width], (1, 1))
        + dot(cols[1], w_self_ref[:, width:], (1, 1))
    )
    for r in range(1, last + 1):
        count_arrives(r)
    master_sum[...] += dot(counts[:masters, :masters], table[...], (1, 0)) + dot(
        counts[:masters, masters:], mirrors[...], (1, 0)
    )
    out_ref[HUBS:, :] = master_sum[HUBS:, :].astype(BF16)
    finish(0)
    each_peer(
        lambda k: copy(
            2, k, returns.at[rows_of(peer(k)), :], returned.at[rows_of(giver(k)), :]
        ).wait_recv()
    )
    hub_sum = lax.fori_loop(
        0,
        parts // batch,
        lambda i, t: t + dot(hits[i], returned[batch_at(i), :], (1, 0)),
        master_sum[:HUBS, :],
    )
    out_ref[:HUBS, :] = hub_sum.astype(BF16)
    finish(1)

    exchange.wait_send()
    for r in range(last + 1):
        across(1 + r, counts.at[count_at(r, half), :], counts.at[count_at(r, half), :]).wait_send()
    each_peer(lambda k: request(k).wait_send())
    each_peer(lambda k: reply(k).wait_send())
    each_peer(lambda k: give_back(k).wait_send())
    for i in range(2):
        each_peer(lambda k: scatter(i, k).wait_send(), low)
        each_peer(lambda k: scatter_high(i, k).wait_send(), high)
        each_peer(lambda k: spread_high(i, k).wait_send(), high)
        each_peer(lambda k: spread(i, k).wait_send(), low)


def on_device(
    features,
    grad_out,
    pre_act,
    neigh_mean,
    w_self,
    w_neigh,
    edge_from,
    edge_to,
    edge_count,
    mirror_master,
    degrees,
):
    masters, width = features.shape
    parts = lax.axis_size("dom")
    mirror_count = mirror_master.shape[0]
    slots = mirror_count // parts
    edges = edge_from.shape[0]
    full = w_self.shape[1]
    weight_rows = 2 * w_self.shape[0]
    low = 2
    while parts % (4 * low) == 0 and 4 * low * low <= parts:
        low *= 2
    low_rows = weight_rows // low
    owners = min(parts // low, low_rows // 16)
    chunk = low_rows // owners
    batch = 8 if parts % 8 == 0 else 1
    block = min(edges, 2048 if masters + mirror_count <= 2048 else 256)
    vmem = pl.BlockSpec(memory_space=pltpu.VMEM)
    anywhere = pl.BlockSpec(memory_space=pl.ANY)
    step = mirror_count // 2
    if (
        masters + mirror_count <= 2048
        and owners * low == parts
        and parts % (LANES // slots) == 0
        and masters % mirror_count == 0
        and edges % 4096 == 0
    ):
        high = owners
        count_block = edges // 2
        weight = jax.ShapeDtypeStruct(w_self.shape, F32)
        return pl.pallas_call(
            functools.partial(count_kernel, parts, low, count_block),
            out_shape=(jax.ShapeDtypeStruct((masters, width), BF16), weight, weight),
            in_specs=[pl.BlockSpec(memory_space=pltpu.SMEM)] + [anywhere] * 10,
            out_specs=(vmem, vmem, vmem),
            scratch_shapes=[
                pltpu.VMEM(features.shape, BF16),
                pltpu.VMEM(features.shape, BF16),
                pltpu.VMEM(features.shape, BF16),
                pltpu.VMEM(features.shape, BF16),
                pltpu.VMEM(w_self.shape, BF16),
                pltpu.VMEM(w_self.shape, BF16),
                pltpu.VMEM((edges // LANES, LANES), jnp.int32),
                pltpu.VMEM((edges // LANES, LANES), jnp.int32),
                pltpu.VMEM((mirror_count // LANES, LANES), jnp.int32),
                pltpu.VMEM((masters // LANES, LANES), jnp.int32),
                pltpu.VMEM((parts, 1, slots), jnp.int32),
                pltpu.VMEM((2, masters, width), BF16),
                pltpu.VMEM((masters, width), BF16),
                pltpu.VMEM((parts, 1, slots), jnp.int32),
                pltpu.VMEM((mirror_count, width), BF16),
                pltpu.VMEM((mirror_count, width), BF16),
                pltpu.VMEM((masters, width), F32),
                pltpu.VMEM((mirror_count, width), BF16),
                pltpu.VMEM((mirror_count, width), BF16),
                pltpu.VMEM((parts // batch, HUBS, batch * slots), BF16),
                pltpu.VMEM((edges // count_block, masters + mirror_count, count_block), F8),
                pltpu.VMEM((step, masters + mirror_count), F32),
                pltpu.VMEM((masters + mirror_count, masters + mirror_count), BF16),
                pltpu.VMEM((2, low, low_rows, width), BF16),
                pltpu.VMEM((2, low, low_rows, width), BF16),
                pltpu.VMEM((2, high, chunk, width), BF16),
                pltpu.VMEM((2, high, chunk, width), BF16),
                pltpu.VMEM((2, high, chunk, width), BF16),
                pltpu.VMEM((2, low, high, chunk, width), BF16),
                pltpu.SemaphoreType.DMA((10,)),
                pltpu.SemaphoreType.DMA((2 + masters // mirror_count,)),
                pltpu.SemaphoreType.DMA((2 + masters // mirror_count,)),
                pltpu.SemaphoreType.DMA((11, parts)),
                pltpu.SemaphoreType.DMA((11, parts)),
            ],
            compiler_params=pltpu.CompilerParams(
                collective_id=1, has_side_effects=True, vmem_limit_bytes=58 * 2**20
            ),
        )(
            edge_count,
            grad_out,
            pre_act,
            features,
            neigh_mean,
            w_self,
            w_neigh,
            edge_from.reshape(-1, LANES),
            edge_to.reshape(-1, LANES),
            mirror_master.reshape(-1, LANES),
            degrees.reshape(-1, LANES),
        )
    input_grad, weights = pl.pallas_call(
        functools.partial(layer_kernel, parts, block),
        out_shape=(
            jax.ShapeDtypeStruct((masters, width), BF16),
            jax.ShapeDtypeStruct((low, owners, chunk, full), BF16),
        ),
        in_specs=[pl.BlockSpec(memory_space=pltpu.SMEM)] + [vmem] * 2 + [anywhere] * 4 + [vmem] * 4,
        out_specs=(vmem, vmem),
        scratch_shapes=[
            pltpu.VMEM(features.shape, BF16),
            pltpu.VMEM(features.shape, BF16),
            pltpu.VMEM(w_self.shape, BF16),
            pltpu.VMEM(w_self.shape, BF16),
            pltpu.VMEM((2, masters, width), BF16),
            pltpu.VMEM((edges // LANES, LANES), jnp.int32),
            pltpu.VMEM((masters, width), BF16),
            pltpu.VMEM((parts, 1, slots), jnp.int32),
            pltpu.VMEM((mirror_count, width), BF16),
            pltpu.VMEM((mirror_count, width), BF16),
            pltpu.VMEM((edges, width), BF16),
            pltpu.VMEM((masters, width), F32),
            pltpu.VMEM((mirror_count, width), F32),
            pltpu.VMEM((mirror_count, width), BF16),
            pltpu.VMEM((mirror_count, width), BF16),
            pltpu.VMEM((parts // batch, HUBS, batch * slots), BF16),
            pltpu.VMEM((low, low_rows, full), BF16),
            pltpu.VMEM((low, low_rows, full), BF16),
            pltpu.VMEM((owners, chunk, full), BF16),
            pltpu.VMEM((parts // low, chunk, full), BF16),
            pltpu.VMEM((owners, chunk, full), BF16),
            pltpu.VMEM((low, owners, chunk, full), BF16),
            pltpu.SemaphoreType.DMA((4,)),
            pltpu.SemaphoreType.DMA((2,)),
            pltpu.SemaphoreType.DMA((7, parts)),
            pltpu.SemaphoreType.DMA((7, parts)),
        ],
        compiler_params=pltpu.CompilerParams(
            collective_id=0, has_side_effects=True, vmem_limit_bytes=60 * 2**20
        ),
    )(
        edge_count,
        grad_out,
        pre_act,
        features,
        neigh_mean,
        w_self,
        w_neigh,
        edge_from.reshape(-1, LANES),
        edge_to.reshape(-1, LANES),
        mirror_master.reshape(parts, 1, slots),
        degrees.reshape(-1, LANES),
    )
    weights = weights.reshape(2, w_self.shape[0], full).astype(F32)
    return (input_grad, weights[0], weights[1])


def solution(mesh):
    placed = (
        P("dom", "feat"),
        P("dom", "feat"),
        P("dom", "feat"),
        P("dom", "feat"),
        P("feat", None),
        P("feat", None),
        P("dom"),
        P("dom"),
        P("dom"),
        P("dom"),
        P("dom"),
    )
    return jax.shard_map(
        on_device,
        mesh=mesh,
        in_specs=placed,
        out_specs=(P("dom", "feat"), P("feat", None), P("feat", None)),
        check_vma=False,
    )
```

```python
import functools

import jax
import jax.numpy as jnp
from jax import lax
from jax.experimental import pallas as pl
from jax.experimental.pallas import tpu as pltpu
from jax.sharding import PartitionSpec as P

LANES = 128
HUBS = 64
MESH = pl.DeviceIdType.MESH
F32, BF16, F8 = jnp.float32, jnp.bfloat16, jnp.float8_e4m3fn


def dot(a, b, over):
    return lax.dot_general(a, b, ((over[:1], over[1:]), ((), ())), preferred_element_type=F32)


def columns_of(row):
    return jnp.transpose(jnp.broadcast_to(row, (LANES, LANES)))


def pick_rows(sinks, first, count):
    one, zero = jnp.ones((), BF16), jnp.zeros((), BF16)
    lane = lax.broadcasted_iota(jnp.int32, (LANES, LANES), 1)
    tiles = []
    for g in range(sinks.shape[0]):
        column = columns_of(sinks[g : g + 1, :])
        tiles.append(
            jnp.concatenate(
                [jnp.where(column == lane + (first + j), one, zero) for j in range(0, count, LANES)],
                axis=1,
            )
        )
    return jnp.concatenate(tiles, axis=0)


def put_rows(sources, first, count):
    one, zero = jnp.ones((), BF16), jnp.zeros((), BF16)
    row = lax.broadcasted_iota(jnp.int32, (count, LANES), 0) + first
    return jnp.concatenate(
        [jnp.where(row == sources[g : g + 1, :], one, zero) for g in range(sources.shape[0])],
        axis=1,
    )


def layer_kernel(
    parts,
    block,
    limit_ref,
    grad_ref,
    pre_ref,
    features_hbm,
    mean_hbm,
    w_self_hbm,
    w_neigh_hbm,
    source_ref,
    sink_ref,
    wanted_ref,
    degree_ref,
    out_ref,
    weights_ref,
    features_ref,
    mean_ref,
    w_self_ref,
    w_neigh_ref,
    cols,
    live,
    table,
    asked,
    replies,
    mirrors,
    picked,
    master_sum,
    mirror_sum,
    returns,
    returned,
    hits,
    partial,
    arrived,
    column_sum,
    column_arrived,
    column_total,
    full,
    load_sems,
    feat_sems,
    send_sems,
    recv_sems,
):
    me, half = lax.axis_index("dom"), lax.axis_index("feat")
    partner = 1 - half
    masters, width = grad_ref.shape
    slots = wanted_ref.shape[2]
    low, low_rows = partial.shape[0], partial.shape[1]
    owners, chunk = column_sum.shape[0], column_sum.shape[1]
    high = parts // low
    at_high, at_low = me // low, lax.rem(me, low)
    groups = block // LANES
    blocks = sink_ref.shape[0] // groups

    def peer(k):
        return lax.rem(me + k, parts)

    def giver(k):
        return lax.rem(me + (parts - k), parts)

    def rows_of(q):
        return pl.ds(pl.multiple_of(q * slots, slots), slots)

    def copy(stage, k, src, dst, device=None):
        return pltpu.make_async_remote_copy(
            src_ref=src,
            dst_ref=dst,
            send_sem=send_sems.at[stage, k],
            recv_sem=recv_sems.at[stage, k],
            device_id={"dom": peer(k) if device is None else device},
            device_id_type=MESH,
        )

    def each_peer(act, count=parts):
        lax.fori_loop(1, count, lambda k, c: (act(k), c)[1], 0)

    loads = [
        pltpu.make_async_copy(src, dst, load_sems.at[i])
        for i, (src, dst) in enumerate(
            (
                (w_neigh_hbm, w_neigh_ref),
                (features_hbm, features_ref),
                (mean_hbm, mean_ref),
                (w_self_hbm, w_self_ref),
            )
        )
    ]

    barrier = pltpu.get_barrier_semaphore()
    pl.semaphore_signal(barrier, inc=1, device_id={"feat": partner}, device_id_type=MESH)
    each_peer(
        lambda k: pl.semaphore_signal(
            barrier, inc=1, device_id={"dom": peer(k)}, device_id_type=MESH
        )
    )
    for load in loads:
        load.start()
    keep = (pre_ref[...] > 0).astype(F32)
    cols[half] = (grad_ref[...].astype(F32) * keep).astype(BF16)
    place = (
        lax.broadcasted_iota(jnp.int32, source_ref.shape, 0) * LANES
        + lax.broadcasted_iota(jnp.int32, source_ref.shape, 1)
    )
    live[...] = jnp.where(place < limit_ref[0], source_ref[...], -1)
    asked[me] = wanted_ref[me]
    pl.semaphore_wait(barrier, parts)

    exchange = pltpu.make_async_remote_copy(
        src_ref=cols.at[half],
        dst_ref=cols.at[half],
        send_sem=feat_sems.at[0],
        recv_sem=feat_sems.at[1],
        device_id={"feat": partner},
        device_id_type=MESH,
    )
    exchange.start()

    def request(k):
        return copy(0, k, wanted_ref.at[peer(k)], asked.at[me])

    each_peer(lambda k: request(k).start())
    def half_at(h):
        return pl.ds(pl.multiple_of(h * width, width), width)

    loads[0].wait()
    own = dot(cols[half], w_neigh_ref[:, half_at(half)], (1, 1))
    pltpu.make_async_remote_copy(
        src_ref=cols.at[half],
        dst_ref=cols.at[partner],
        send_sem=feat_sems.at[0],
        recv_sem=feat_sems.at[1],
        device_id={"feat": partner},
        device_id_type=MESH,
    ).wait_recv()

    both = jnp.concatenate([cols[0], cols[1]], axis=1)
    per_weight = low // 2
    for i, operand in enumerate((features_ref, mean_ref)):
        loads[1 + i].wait()
        part = dot(operand[...], both, (0, 0)).astype(BF16)
        for c in range(per_weight):
            partial[i * per_weight + c] = part[c * low_rows : (c + 1) * low_rows, :]

    def low_peer(k):
        return lax.rem(at_low + k, low)

    def low_giver(k):
        return lax.rem(at_low + (low - k), low)

    def high_peer(k):
        return lax.rem(at_high + k, high)

    def high_giver(k):
        return lax.rem(at_high + (high - k), high)

    def to_low(stage, k, src, dst):
        return copy(stage, k, src, dst, at_high * low + low_peer(k))

    def to_high(stage, k, src, dst):
        return copy(stage, k, src, dst, high_peer(k) * low + at_low)

    def guarded(act, owner):
        if owners == high:
            return act
        return lambda k: pl.when(owner(k) < owners)(lambda: act(k))

    def if_owner(act):
        if owners == high:
            act()
        else:
            pl.when(at_high < owners)(act)

    def scatter(k):
        return to_low(2, k, partial.at[low_peer(k)], arrived.at[at_low])

    each_peer(lambda k: scatter(k).start(), low)
    neigh = own + dot(cols[partner], w_neigh_ref[:, half_at(partner)], (1, 1))
    for g in range(masters // LANES):
        at = slice(g * LANES, (g + 1) * LANES)
        degree = columns_of(degree_ref[g : g + 1, :]).astype(F32)
        degree = jnp.concatenate([degree] * (width // LANES), axis=1)
        table[at, :] = (neigh[at, :] / degree).astype(BF16)

    each_peer(lambda k: copy(0, k, wanted_ref.at[peer(k)], asked.at[giver(k)]).wait_recv())

    batch = 8 if parts % 8 == 0 else 1
    hub = lax.broadcasted_iota(jnp.int32, (HUBS, slots), 0)

    def batch_at(i):
        return pl.ds(pl.multiple_of(i * batch * slots, batch * slots), batch * slots)

    def answer(i, c):
        hit = jnp.concatenate(
            [
                jnp.where(hub == asked[i * batch + j], jnp.ones((), BF16), jnp.zeros((), BF16))
                for j in range(batch)
            ],
            axis=1,
        )
        hits[i] = hit
        replies[batch_at(i), :] = dot(hit, table[:HUBS, :], (0, 0)).astype(BF16)
        return c

    lax.fori_loop(0, parts // batch, answer, 0)
    mirrors[rows_of(me), :] = replies[rows_of(me), :]

    def reply(k):
        return copy(1, k, replies.at[rows_of(peer(k)), :], mirrors.at[rows_of(me), :])

    each_peer(lambda k: reply(k).start())

    def block_at(b):
        return pl.ds(pl.multiple_of(b * groups, groups), groups)

    def edges_at(b):
        return pl.ds(pl.multiple_of(b * block, block), block)

    def from_masters(b, c):
        pick = pick_rows(sink_ref[block_at(b), :], 0, masters)
        picked[edges_at(b), :] = dot(pick, table[...], (1, 0)).astype(BF16)
        return c

    lax.fori_loop(0, blocks, from_masters, 0)

    each_peer(
        lambda k: to_low(2, k, partial.at[low_peer(k)], arrived.at[low_giver(k)]).wait_recv(), low
    )
    total = lax.fori_loop(
        1,
        low,
        lambda k, t: t + arrived[low_giver(k)].astype(F32),
        partial[at_low].astype(F32),
    ).astype(BF16)
    for c in range(owners):
        column_sum[c] = total[c * chunk : (c + 1) * chunk, :]

    def column_place():
        return lax.rem(at_high, owners)

    def scatter_high(k):
        return to_high(
            4, k, column_sum.at[lax.rem(high_peer(k), owners)], column_arrived.at[at_high]
        )

    each_peer(guarded(lambda k: scatter_high(k).start(), high_peer), high)

    each_peer(
        lambda k: copy(
            1, k, replies.at[rows_of(peer(k)), :], mirrors.at[rows_of(giver(k)), :]
        ).wait_recv()
    )
    mirror_sum[...] = jnp.zeros_like(mirror_sum)
    mirror_count = mirrors.shape[0]

    def from_mirrors(b, c):
        pick = pick_rows(sink_ref[block_at(b), :], masters, mirror_count)
        more = dot(pick, mirrors[...], (1, 0)).astype(BF16)
        row = picked[edges_at(b), :] + more
        picked[edges_at(b), :] = row
        return c

    lax.fori_loop(0, blocks, from_mirrors, 0)

    def column_spread(k):
        return to_high(5, k, column_total.at[column_place()], column_total.at[column_place()])

    def reduce_column():
        each_peer(
            lambda k: to_high(
                4,
                k,
                column_sum.at[lax.rem(high_peer(k), owners)],
                column_arrived.at[high_giver(k)],
            ).wait_recv(),
            high,
        )
        column_total[column_place()] = lax.fori_loop(
            1,
            high,
            lambda k, t: t + column_arrived[high_giver(k)].astype(F32),
            column_sum[column_place()].astype(F32),
        ).astype(BF16)
        each_peer(lambda k: column_spread(k).start(), high)

    if_owner(reduce_column)

    def to_mirrors(b, c):
        put = put_rows(live[block_at(b), :], masters, mirror_count)
        mirror_sum[...] += dot(put, picked[edges_at(b), :], (1, 0))
        return c

    lax.fori_loop(0, blocks, to_mirrors, 0)
    returns[...] = mirror_sum[...].astype(BF16)
    returned[rows_of(me), :] = returns[rows_of(me), :]

    def give_back(k):
        return copy(3, k, returns.at[rows_of(peer(k)), :], returned.at[rows_of(me), :])

    each_peer(lambda k: give_back(k).start())

    each_peer(
        guarded(
            lambda k: to_high(
                5,
                k,
                column_total.at[column_place()],
                column_total.at[lax.rem(high_giver(k), owners)],
            ).wait_recv(),
            high_giver,
        ),
        high,
    )
    full[at_low] = column_total[...]

    def spread(k):
        return to_low(6, k, column_total, full.at[at_low])

    each_peer(lambda k: spread(k).start(), low)

    loads[3].wait()
    master_sum[...] = dot(cols[0], w_self_ref[:, :width], (1, 1)) + dot(
        cols[1], w_self_ref[:, width:], (1, 1)
    )

    def to_masters(b, c):
        put = put_rows(live[block_at(b), :], 0, masters)
        master_sum[...] += dot(put, picked[edges_at(b), :], (1, 0))
        return c

    lax.fori_loop(0, blocks, to_masters, 0)

    each_peer(
        lambda k: copy(
            3, k, returns.at[rows_of(peer(k)), :], returned.at[rows_of(giver(k)), :]
        ).wait_recv()
    )
    hub_sum = lax.fori_loop(
        0,
        parts // batch,
        lambda i, t: t + dot(hits[i], returned[batch_at(i), :], (1, 0)),
        master_sum[:HUBS, :],
    )
    out_ref[:HUBS, :] = hub_sum.astype(BF16)
    out_ref[HUBS:, :] = master_sum[HUBS:, :].astype(BF16)

    each_peer(lambda k: to_low(6, k, column_total, full.at[low_giver(k)]).wait_recv(), low)
    weights_ref[...] = full[...]

    exchange.wait_send()
    each_peer(lambda k: request(k).wait_send())
    each_peer(lambda k: reply(k).wait_send())
    each_peer(lambda k: give_back(k).wait_send())
    each_peer(lambda k: scatter(k).wait_send(), low)
    each_peer(guarded(lambda k: scatter_high(k).wait_send(), high_peer), high)
    if_owner(lambda: each_peer(lambda k: column_spread(k).wait_send(), high))
    each_peer(lambda k: spread(k).wait_send(), low)


def ones_at(index, count, first):
    one, zero = jnp.ones((), BF16), jnp.zeros((), BF16)
    row = (lax.broadcasted_iota(jnp.int32, (count, LANES), 0) + first).astype(jnp.int16)
    index = index.astype(jnp.int16)
    return jnp.concatenate(
        [
            jnp.where(row == index[g : g + 1, :], one, zero).astype(F8)
            for g in range(index.shape[0])
        ],
        axis=1,
    )


def count_kernel(
    parts,
    low,
    block,
    limit_ref,
    grad_hbm,
    pre_hbm,
    features_hbm,
    mean_hbm,
    w_self_hbm,
    w_neigh_hbm,
    source_hbm,
    sink_hbm,
    wanted_hbm,
    degree_hbm,
    out_ref,
    weights_ref,
    grads,
    operands,
    w_self_ref,
    w_neigh_ref,
    edges,
    asking,
    degree_ref,
    wanted,
    cols,
    table,
    asked,
    replies,
    mirrors,
    master_sum,
    returns,
    returned,
    hits,
    sinks,
    count_sum,
    counts,
    partial,
    arrived,
    column_sum,
    column_arrived,
    column_total,
    full,
    load_sems,
    feat_send,
    feat_recv,
    send_sems,
    recv_sems,
):
    me, half = lax.axis_index("dom"), lax.axis_index("feat")
    partner = 1 - half
    masters, width = out_ref.shape
    slots = wanted.shape[2]
    mirror_count = mirrors.shape[0]
    rows = masters + mirror_count
    low_rows = partial.shape[2]
    high, chunk = column_sum.shape[1], column_sum.shape[2]
    at_high, at_low = me // low, lax.rem(me, low)
    groups = block // LANES
    blocks = sinks.shape[0]
    step = mirror_count // 2
    column_halves = (half, partner)
    source_ref, sink_ref = edges.at[0], edges.at[1]

    def peer(k):
        return lax.rem(me + k, parts)

    def rows_of(q):
        return pl.ds(pl.multiple_of(q * slots, slots), slots)

    def half_at(h):
        return pl.ds(pl.multiple_of(h * width, width), width)

    def copy(stage, src, dst, device):
        return pltpu.make_async_remote_copy(
            src_ref=src,
            dst_ref=dst,
            send_sem=send_sems.at[stage],
            recv_sem=recv_sems.at[stage],
            device_id={"dom": device},
            device_id_type=MESH,
        )

    def all_of(stage, ref):
        return copy(stage, ref, ref, peer(1))

    def across(i, src, dst):
        return pltpu.make_async_remote_copy(
            src_ref=src,
            dst_ref=dst,
            send_sem=feat_send.at[i],
            recv_sem=feat_recv.at[i],
            device_id={"feat": partner},
            device_id_type=MESH,
        )

    def each_peer(act, count=parts):
        lax.fori_loop(1, count, lambda k, c: (act(k), c)[1], 0)

    def load(i, *pairs):
        for src, dst in pairs:
            pltpu.make_async_copy(src, dst, load_sems.at[i]).start()

    def loaded(i, ref):
        pltpu.make_async_copy(ref, ref, load_sems.at[i]).wait()

    barrier = pltpu.get_barrier_semaphore()
    pl.semaphore_signal(barrier, inc=1, device_id={"feat": partner}, device_id_type=MESH)
    each_peer(
        lambda k: pl.semaphore_signal(
            barrier, inc=1, device_id={"dom": peer(k)}, device_id_type=MESH
        )
    )
    load(0, (grad_hbm, grads.at[0]), (pre_hbm, grads.at[1]))
    load(1, (features_hbm, operands.at[0]), (mean_hbm, operands.at[1]))
    load(2, (wanted_hbm, asking))
    load(3, (source_hbm, edges.at[0]), (sink_hbm, edges.at[1]))
    load(4, (w_neigh_hbm, w_neigh_ref))
    load(5, (degree_hbm, degree_ref))
    load(6, (w_self_hbm, w_self_ref))
    loaded(0, grads)
    keep = (grads[1] > 0).astype(F32)
    cols[half] = (grads[0].astype(F32) * keep).astype(BF16)

    per_weight = low // 2

    def weigh(h):
        for i in range(2):
            part = dot(operands[i], cols[h], (0, 0)).astype(BF16)
            for c in range(per_weight):
                partial[h, i * per_weight + c] = part[c * low_rows : (c + 1) * low_rows, :]

    def low_peer(k):
        return lax.rem(at_low + k, low)

    def low_giver(k):
        return lax.rem(at_low + (low - k), low)

    def high_peer(k):
        return lax.rem(at_high + k, high)

    def high_giver(k):
        return lax.rem(at_high + (high - k), high)

    def to_low(stage, k, src, dst):
        return copy(stage, src, dst, at_high * low + low_peer(k))

    def to_high(stage, k, src, dst):
        return copy(stage, src, dst, high_peer(k) * low + at_low)

    def scatter(i, k):
        h = column_halves[i]
        return to_low(3 + i, k, partial.at[h, low_peer(k)], arrived.at[h, at_low])

    def scatter_high(i, k):
        h = column_halves[i]
        return to_high(5 + i, k, column_sum.at[h, high_peer(k)], column_arrived.at[h, at_high])

    def spread_high(i, k):
        h = column_halves[i]
        return to_high(7 + i, k, column_total.at[h, at_high], column_total.at[h, at_high])

    def spread(i, k):
        h = column_halves[i]
        return to_low(9 + i, k, column_total.at[h], full.at[h, at_low])

    def low_batch(ref, i):
        return ref.at[column_halves[i], pl.ds(0, low - 1)]

    def high_batch(ref, i):
        return ref.at[column_halves[i], pl.ds(0, high - 1)]

    def add_low(i):
        h = column_halves[i]
        all_of(3 + i, low_batch(arrived, i)).wait_recv()
        total = partial[h, at_low].astype(F32)
        for k in range(1, low):
            total = total + arrived[h, low_giver(k)].astype(F32)
        total = total.astype(BF16)
        for c in range(high):
            column_sum[h, c] = total[c * chunk : (c + 1) * chunk, :]
        each_peer(lambda k: scatter_high(i, k).start(), high)

    def add_high(i):
        h = column_halves[i]
        all_of(5 + i, high_batch(column_arrived, i)).wait_recv()
        total = column_sum[h, at_high].astype(F32)
        for k in range(1, high):
            total = total + column_arrived[h, high_giver(k)].astype(F32)
        column_total[h, at_high] = total.astype(BF16)
        each_peer(lambda k: spread_high(i, k).start(), high)

    def pass_on(i):
        h = column_halves[i]
        all_of(7 + i, high_batch(column_total, i)).wait_recv()
        each_peer(lambda k: spread(i, k).start(), low)
        full[h, at_low] = column_total[h]

    def finish(i):
        h = column_halves[i]
        all_of(9 + i, low_batch(full, i)).wait_recv()
        weights_ref[h] = full[h]

    def block_at(b):
        return pl.ds(b * groups, groups)

    def lay_sinks(b):
        sinks[b] = ones_at(sink_ref[block_at(b), :], rows, 0)

    loaded(1, operands)
    weigh(half)
    loaded(2, asking)
    per_row = LANES // slots
    for p in range(parts):
        at = (p % per_row) * slots
        wanted[p] = asking[p // per_row : p // per_row + 1, at : at + slots]
    asked[me] = wanted[me]
    loaded(3, edges)
    place = (
        lax.broadcasted_iota(jnp.int32, source_ref.shape, 0) * LANES
        + lax.broadcasted_iota(jnp.int32, source_ref.shape, 1)
    )
    source_ref[...] = jnp.where(place < limit_ref[0], source_ref[...], -1)
    lay_sinks(0)
    pl.semaphore_wait(barrier, parts)

    exchange = across(0, cols.at[half], cols.at[half])
    exchange.start()

    def request(k):
        return copy(0, wanted.at[peer(k)], asked.at[me], peer(k))

    def reply(k):
        return copy(1, replies.at[rows_of(peer(k)), :], mirrors.at[rows_of(me), :], peer(k))

    def give_back(k):
        return copy(2, returns.at[rows_of(peer(k)), :], returned.at[rows_of(me), :], peer(k))

    others = pl.ds(0, (parts - 1) * slots)
    each_peer(lambda k: request(k).start())
    each_peer(lambda k: scatter(0, k).start(), low)
    loaded(4, w_neigh_ref)
    loaded(5, degree_ref)
    own = dot(cols[half], w_neigh_ref[:, half_at(half)], (1, 1))
    for b in range(1, blocks):
        lay_sinks(b)
    across(0, cols.at[half], cols.at[partner]).wait_recv()
    weigh(partner)
    each_peer(lambda k: scatter(1, k).start(), low)

    neigh = own + dot(cols[partner], w_neigh_ref[:, half_at(partner)], (1, 1))
    for g in range(masters // LANES):
        at = slice(g * LANES, (g + 1) * LANES)
        degree = columns_of(degree_ref[g : g + 1, :]).astype(F32)
        degree = jnp.concatenate([degree] * (width // LANES), axis=1)
        table[at, :] = (neigh[at, :] / degree).astype(BF16)

    all_of(0, asked.at[pl.ds(0, parts - 1)]).wait_recv()

    batch = 8 if parts % 8 == 0 else 1
    hub = lax.broadcasted_iota(jnp.int32, (HUBS, slots), 0)

    def batch_at(i):
        return pl.ds(pl.multiple_of(i * batch * slots, batch * slots), batch * slots)

    def answer(i, c):
        hit = jnp.concatenate(
            [
                jnp.where(hub == asked[i * batch + j], jnp.ones((), BF16), jnp.zeros((), BF16))
                for j in range(batch)
            ],
            axis=1,
        )
        hits[i] = hit
        replies[batch_at(i), :] = dot(hit, table[:HUBS, :], (0, 0)).astype(BF16)
        return c

    lax.fori_loop(0, parts // batch, answer, 0)
    each_peer(lambda k: reply(k).start())
    mirrors[rows_of(me), :] = replies[rows_of(me), :]

    def count_at(r, h):
        first = masters + h * step if r == 0 else h * (masters // 2) + (r - 1) * step
        return pl.ds(pl.multiple_of(first, step), step)

    def count(r, b):
        first = masters + half * step if r == 0 else half * (masters // 2) + (r - 1) * step
        source = ones_at(source_ref[block_at(b), :], step, first)
        term = dot(source, sinks[b], (1, 1))
        if b > 0:
            term = count_sum[...] + term
        if b < blocks - 1:
            count_sum[...] = term
            return
        counts[count_at(r, half), :] = term.astype(BF16)
        across(1 + r, counts.at[count_at(r, half), :], counts.at[count_at(r, half), :]).start()

    def count_arrives(r):
        across(1 + r, counts.at[count_at(r, half), :], counts.at[count_at(r, partner), :]).wait_recv()

    def return_mirrors():
        count_arrives(0)
        own_part = dot(counts[masters:, :masters], table[...], (1, 0))
        all_of(1, mirrors.at[others, :]).wait_recv()
        mirror_sum = own_part + dot(counts[masters:, masters:], mirrors[...], (1, 0))
        returns[...] = mirror_sum.astype(BF16)
        each_peer(lambda k: give_back(k).start())
        returned[rows_of(me), :] = returns[rows_of(me), :]

    last = masters // mirror_count
    acts = [
        lambda: add_low(0),
        lambda: add_low(1),
        lambda: add_high(0),
        lambda: add_high(1),
        return_mirrors,
        lambda: pass_on(0),
        lambda: pass_on(1),
    ]
    plan = {0: (0,), 1: (1,), 2: (2,), 3: (3, 4), 4: (5,), 5: (6,), "mid": ()}
    for unit in range((last + 1) * blocks):
        count(unit // blocks, unit % blocks)
        for a in plan.get(unit, ()):
            acts[a]()
    loaded(6, w_self_ref)
    master_sum[...] = (
        dot(cols[0], w_self_ref[:, :width], (1, 1))
        + dot(cols[1], w_self_ref[:, width:], (1, 1))
    )
    for a in plan["mid"]:
        acts[a]()
    for r in range(1, last + 1):
        count_arrives(r)
    master_sum[...] += dot(counts[:masters, :masters], table[...], (1, 0)) + dot(
        counts[:masters, masters:], mirrors[...], (1, 0)
    )
    out_ref[HUBS:, :] = master_sum[HUBS:, :].astype(BF16)
    all_of(2, returned.at[others, :]).wait_recv()
    hub_sum = lax.fori_loop(
        0,
        parts // batch,
        lambda i, t: t + dot(hits[i], returned[batch_at(i), :], (1, 0)),
        master_sum[:HUBS, :],
    )
    out_ref[:HUBS, :] = hub_sum.astype(BF16)
    finish(0)
    finish(1)

    exchange.wait_send()
    for r in range(last + 1):
        across(1 + r, counts.at[count_at(r, half), :], counts.at[count_at(r, half), :]).wait_send()
    all_of(0, wanted.at[pl.ds(0, parts - 1)]).wait_send()
    all_of(1, replies.at[others, :]).wait_send()
    all_of(2, returns.at[others, :]).wait_send()
    for i in range(2):
        all_of(3 + i, low_batch(partial, i)).wait_send()
        all_of(5 + i, high_batch(column_sum, i)).wait_send()
        all_of(7 + i, high_batch(column_total, i)).wait_send()
        all_of(9 + i, low_batch(full, i)).wait_send()


def settle_kernel(grad_ref, weights_ref, out_ref, self_ref, neigh_ref):
    out_ref[...] = grad_ref[...]
    halves, low, high, chunk, width = weights_ref.shape
    for w, ref in enumerate((self_ref, neigh_ref)):
        for h in range(halves):
            for c in range(low // 2):
                block = weights_ref[h, w * (low // 2) + c].reshape(high * chunk, width)
                ref[
                    c * high * chunk : (c + 1) * high * chunk, h * width : (h + 1) * width
                ] = block.astype(F32)


def on_device(
    features,
    grad_out,
    pre_act,
    neigh_mean,
    w_self,
    w_neigh,
    edge_from,
    edge_to,
    edge_count,
    mirror_master,
    degrees,
):
    masters, width = features.shape
    parts = lax.axis_size("dom")
    mirror_count = mirror_master.shape[0]
    slots = mirror_count // parts
    edges = edge_from.shape[0]
    full = w_self.shape[1]
    weight_rows = 2 * w_self.shape[0]
    low = 2
    while parts % (4 * low) == 0 and 4 * low * low <= parts:
        low *= 2
    low_rows = weight_rows // low
    owners = min(parts // low, low_rows // 16)
    chunk = low_rows // owners
    batch = 8 if parts % 8 == 0 else 1
    block = min(edges, 2048 if masters + mirror_count <= 2048 else 256)
    vmem = pl.BlockSpec(memory_space=pltpu.VMEM)
    anywhere = pl.BlockSpec(memory_space=pl.ANY)
    step = mirror_count // 2
    if (
        masters + mirror_count <= 2048
        and owners * low == parts
        and parts % (LANES // slots) == 0
        and masters % mirror_count == 0
        and edges % 4096 == 0
    ):
        high = owners
        count_block = edges // 2
        weight = jax.ShapeDtypeStruct(w_self.shape, F32)
        rows = masters + mirror_count
        sent = pl.pallas_call(
            functools.partial(count_kernel, parts, low, count_block),
            out_shape=(
                pltpu.VMEM((masters, width), BF16),
                pltpu.VMEM((2, low, high, chunk, width), BF16),
            ),
            in_specs=[pl.BlockSpec(memory_space=pltpu.SMEM)] + [anywhere] * 10,
            out_specs=(vmem, vmem),
            scratch_shapes=[
                pltpu.VMEM((2, masters, width), BF16),
                pltpu.VMEM((2, masters, width), BF16),
                pltpu.VMEM(w_self.shape, BF16),
                pltpu.VMEM(w_self.shape, BF16),
                pltpu.VMEM((2, edges // LANES, LANES), jnp.int32),
                pltpu.VMEM((mirror_count // LANES, LANES), jnp.int32),
                pltpu.VMEM((masters // LANES, LANES), jnp.int32),
                pltpu.VMEM((parts, 1, slots), jnp.int32),
                pltpu.VMEM((2, masters, width), BF16),
                pltpu.VMEM((masters, width), BF16),
                pltpu.VMEM((parts, 1, slots), jnp.int32),
                pltpu.VMEM((mirror_count, width), BF16),
                pltpu.VMEM((mirror_count, width), BF16),
                pltpu.VMEM((masters, width), F32),
                pltpu.VMEM((mirror_count, width), BF16),
                pltpu.VMEM((mirror_count, width), BF16),
                pltpu.VMEM((parts // batch, HUBS, batch * slots), BF16),
                pltpu.VMEM((edges // count_block, rows, count_block), F8),
                pltpu.VMEM((step, rows), F32),
                pltpu.VMEM((rows, rows), BF16),
                pltpu.VMEM((2, low, low_rows, width), BF16),
                pltpu.VMEM((2, low, low_rows, width), BF16),
                pltpu.VMEM((2, high, chunk, width), BF16),
                pltpu.VMEM((2, high, chunk, width), BF16),
                pltpu.VMEM((2, high, chunk, width), BF16),
                pltpu.VMEM((2, low, high, chunk, width), BF16),
                pltpu.SemaphoreType.DMA((7,)),
                pltpu.SemaphoreType.DMA((2 + masters // mirror_count,)),
                pltpu.SemaphoreType.DMA((2 + masters // mirror_count,)),
                pltpu.SemaphoreType.DMA((11,)),
                pltpu.SemaphoreType.DMA((11,)),
            ],
            compiler_params=pltpu.CompilerParams(
                collective_id=1, has_side_effects=True, vmem_limit_bytes=54 * 2**20
            ),
        )(
            edge_count,
            grad_out,
            pre_act,
            features,
            neigh_mean,
            w_self,
            w_neigh,
            edge_from.reshape(-1, LANES),
            edge_to.reshape(-1, LANES),
            mirror_master.reshape(-1, LANES),
            degrees.reshape(-1, LANES),
        )
        return pl.pallas_call(
            settle_kernel,
            out_shape=(jax.ShapeDtypeStruct((masters, width), BF16), weight, weight),
            in_specs=[vmem] * 2,
            out_specs=(vmem,) * 3,
        )(*[pltpu.with_memory_space_constraint(x, pltpu.VMEM) for x in sent])
    input_grad, weights = pl.pallas_call(
        functools.partial(layer_kernel, parts, block),
        out_shape=(
            jax.ShapeDtypeStruct((masters, width), BF16),
            jax.ShapeDtypeStruct((low, owners, chunk, full), BF16),
        ),
        in_specs=[pl.BlockSpec(memory_space=pltpu.SMEM)] + [vmem] * 2 + [anywhere] * 4 + [vmem] * 4,
        out_specs=(vmem, vmem),
        scratch_shapes=[
            pltpu.VMEM(features.shape, BF16),
            pltpu.VMEM(features.shape, BF16),
            pltpu.VMEM(w_self.shape, BF16),
            pltpu.VMEM(w_self.shape, BF16),
            pltpu.VMEM((2, masters, width), BF16),
            pltpu.VMEM((edges // LANES, LANES), jnp.int32),
            pltpu.VMEM((masters, width), BF16),
            pltpu.VMEM((parts, 1, slots), jnp.int32),
            pltpu.VMEM((mirror_count, width), BF16),
            pltpu.VMEM((mirror_count, width), BF16),
            pltpu.VMEM((edges, width), BF16),
            pltpu.VMEM((masters, width), F32),
            pltpu.VMEM((mirror_count, width), F32),
            pltpu.VMEM((mirror_count, width), BF16),
            pltpu.VMEM((mirror_count, width), BF16),
            pltpu.VMEM((parts // batch, HUBS, batch * slots), BF16),
            pltpu.VMEM((low, low_rows, full), BF16),
            pltpu.VMEM((low, low_rows, full), BF16),
            pltpu.VMEM((owners, chunk, full), BF16),
            pltpu.VMEM((parts // low, chunk, full), BF16),
            pltpu.VMEM((owners, chunk, full), BF16),
            pltpu.VMEM((low, owners, chunk, full), BF16),
            pltpu.SemaphoreType.DMA((4,)),
            pltpu.SemaphoreType.DMA((2,)),
            pltpu.SemaphoreType.DMA((7, parts)),
            pltpu.SemaphoreType.DMA((7, parts)),
        ],
        compiler_params=pltpu.CompilerParams(
            collective_id=0, has_side_effects=True, vmem_limit_bytes=60 * 2**20
        ),
    )(
        edge_count,
        grad_out,
        pre_act,
        features,
        neigh_mean,
        w_self,
        w_neigh,
        edge_from.reshape(-1, LANES),
        edge_to.reshape(-1, LANES),
        mirror_master.reshape(parts, 1, slots),
        degrees.reshape(-1, LANES),
    )
    weights = weights.reshape(2, w_self.shape[0], full).astype(F32)
    return (input_grad, weights[0], weights[1])


def solution(mesh):
    placed = (
        P("dom", "feat"),
        P("dom", "feat"),
        P("dom", "feat"),
        P("dom", "feat"),
        P("feat", None),
        P("feat", None),
        P("dom"),
        P("dom"),
        P("dom"),
        P("dom"),
        P("dom"),
    )
    return jax.shard_map(
        on_device,
        mesh=mesh,
        in_specs=placed,
        out_specs=(P("dom", "feat"), P("feat", None), P("feat", None)),
        check_vma=False,
    )
```

```python
import functools

import jax
import jax.numpy as jnp
from jax import lax
from jax.experimental import pallas as pl
from jax.experimental.pallas import tpu as pltpu
from jax.sharding import PartitionSpec as P

LANES = 128
HUBS = 64
MESH = pl.DeviceIdType.MESH
F32, BF16, F8 = jnp.float32, jnp.bfloat16, jnp.float8_e4m3fn


def dot(a, b, over):
    return lax.dot_general(a, b, ((over[:1], over[1:]), ((), ())), preferred_element_type=F32)


def columns_of(row):
    return jnp.transpose(jnp.broadcast_to(row, (LANES, LANES)))


def pick_rows(sinks, first, count):
    one, zero = jnp.ones((), BF16), jnp.zeros((), BF16)
    lane = lax.broadcasted_iota(jnp.int32, (LANES, LANES), 1)
    tiles = []
    for g in range(sinks.shape[0]):
        column = columns_of(sinks[g : g + 1, :])
        tiles.append(
            jnp.concatenate(
                [jnp.where(column == lane + (first + j), one, zero) for j in range(0, count, LANES)],
                axis=1,
            )
        )
    return jnp.concatenate(tiles, axis=0)


def put_rows(sources, first, count):
    one, zero = jnp.ones((), BF16), jnp.zeros((), BF16)
    row = lax.broadcasted_iota(jnp.int32, (count, LANES), 0) + first
    return jnp.concatenate(
        [jnp.where(row == sources[g : g + 1, :], one, zero) for g in range(sources.shape[0])],
        axis=1,
    )


def layer_kernel(
    parts,
    block,
    limit_ref,
    grad_ref,
    pre_ref,
    features_hbm,
    mean_hbm,
    w_self_hbm,
    w_neigh_hbm,
    source_ref,
    sink_ref,
    wanted_ref,
    degree_ref,
    out_ref,
    weights_ref,
    features_ref,
    mean_ref,
    w_self_ref,
    w_neigh_ref,
    cols,
    live,
    table,
    asked,
    replies,
    mirrors,
    picked,
    master_sum,
    mirror_sum,
    returns,
    returned,
    hits,
    partial,
    arrived,
    column_sum,
    column_arrived,
    column_total,
    full,
    load_sems,
    feat_sems,
    send_sems,
    recv_sems,
):
    me, half = lax.axis_index("dom"), lax.axis_index("feat")
    partner = 1 - half
    masters, width = grad_ref.shape
    slots = wanted_ref.shape[2]
    low, low_rows = partial.shape[0], partial.shape[1]
    owners, chunk = column_sum.shape[0], column_sum.shape[1]
    high = parts // low
    at_high, at_low = me // low, lax.rem(me, low)
    groups = block // LANES
    blocks = sink_ref.shape[0] // groups

    def peer(k):
        return lax.rem(me + k, parts)

    def giver(k):
        return lax.rem(me + (parts - k), parts)

    def rows_of(q):
        return pl.ds(pl.multiple_of(q * slots, slots), slots)

    def copy(stage, k, src, dst, device=None):
        return pltpu.make_async_remote_copy(
            src_ref=src,
            dst_ref=dst,
            send_sem=send_sems.at[stage, k],
            recv_sem=recv_sems.at[stage, k],
            device_id={"dom": peer(k) if device is None else device},
            device_id_type=MESH,
        )

    def each_peer(act, count=parts):
        lax.fori_loop(1, count, lambda k, c: (act(k), c)[1], 0)

    loads = [
        pltpu.make_async_copy(src, dst, load_sems.at[i])
        for i, (src, dst) in enumerate(
            (
                (w_neigh_hbm, w_neigh_ref),
                (features_hbm, features_ref),
                (mean_hbm, mean_ref),
                (w_self_hbm, w_self_ref),
            )
        )
    ]

    barrier = pltpu.get_barrier_semaphore()
    pl.semaphore_signal(barrier, inc=1, device_id={"feat": partner}, device_id_type=MESH)
    each_peer(
        lambda k: pl.semaphore_signal(
            barrier, inc=1, device_id={"dom": peer(k)}, device_id_type=MESH
        )
    )
    for load in loads:
        load.start()
    keep = (pre_ref[...] > 0).astype(F32)
    cols[half] = (grad_ref[...].astype(F32) * keep).astype(BF16)
    place = (
        lax.broadcasted_iota(jnp.int32, source_ref.shape, 0) * LANES
        + lax.broadcasted_iota(jnp.int32, source_ref.shape, 1)
    )
    live[...] = jnp.where(place < limit_ref[0], source_ref[...], -1)
    asked[me] = wanted_ref[me]
    pl.semaphore_wait(barrier, parts)

    exchange = pltpu.make_async_remote_copy(
        src_ref=cols.at[half],
        dst_ref=cols.at[half],
        send_sem=feat_sems.at[0],
        recv_sem=feat_sems.at[1],
        device_id={"feat": partner},
        device_id_type=MESH,
    )
    exchange.start()

    def request(k):
        return copy(0, k, wanted_ref.at[peer(k)], asked.at[me])

    each_peer(lambda k: request(k).start())
    def half_at(h):
        return pl.ds(pl.multiple_of(h * width, width), width)

    loads[0].wait()
    own = dot(cols[half], w_neigh_ref[:, half_at(half)], (1, 1))
    pltpu.make_async_remote_copy(
        src_ref=cols.at[half],
        dst_ref=cols.at[partner],
        send_sem=feat_sems.at[0],
        recv_sem=feat_sems.at[1],
        device_id={"feat": partner},
        device_id_type=MESH,
    ).wait_recv()

    both = jnp.concatenate([cols[0], cols[1]], axis=1)
    per_weight = low // 2
    for i, operand in enumerate((features_ref, mean_ref)):
        loads[1 + i].wait()
        part = dot(operand[...], both, (0, 0)).astype(BF16)
        for c in range(per_weight):
            partial[i * per_weight + c] = part[c * low_rows : (c + 1) * low_rows, :]

    def low_peer(k):
        return lax.rem(at_low + k, low)

    def low_giver(k):
        return lax.rem(at_low + (low - k), low)

    def high_peer(k):
        return lax.rem(at_high + k, high)

    def high_giver(k):
        return lax.rem(at_high + (high - k), high)

    def to_low(stage, k, src, dst):
        return copy(stage, k, src, dst, at_high * low + low_peer(k))

    def to_high(stage, k, src, dst):
        return copy(stage, k, src, dst, high_peer(k) * low + at_low)

    def guarded(act, owner):
        if owners == high:
            return act
        return lambda k: pl.when(owner(k) < owners)(lambda: act(k))

    def if_owner(act):
        if owners == high:
            act()
        else:
            pl.when(at_high < owners)(act)

    def scatter(k):
        return to_low(2, k, partial.at[low_peer(k)], arrived.at[at_low])

    each_peer(lambda k: scatter(k).start(), low)
    neigh = own + dot(cols[partner], w_neigh_ref[:, half_at(partner)], (1, 1))
    for g in range(masters // LANES):
        at = slice(g * LANES, (g + 1) * LANES)
        degree = columns_of(degree_ref[g : g + 1, :]).astype(F32)
        degree = jnp.concatenate([degree] * (width // LANES), axis=1)
        table[at, :] = (neigh[at, :] / degree).astype(BF16)

    each_peer(lambda k: copy(0, k, wanted_ref.at[peer(k)], asked.at[giver(k)]).wait_recv())

    batch = 8 if parts % 8 == 0 else 1
    hub = lax.broadcasted_iota(jnp.int32, (HUBS, slots), 0)

    def batch_at(i):
        return pl.ds(pl.multiple_of(i * batch * slots, batch * slots), batch * slots)

    def answer(i, c):
        hit = jnp.concatenate(
            [
                jnp.where(hub == asked[i * batch + j], jnp.ones((), BF16), jnp.zeros((), BF16))
                for j in range(batch)
            ],
            axis=1,
        )
        hits[i] = hit
        replies[batch_at(i), :] = dot(hit, table[:HUBS, :], (0, 0)).astype(BF16)
        return c

    lax.fori_loop(0, parts // batch, answer, 0)
    mirrors[rows_of(me), :] = replies[rows_of(me), :]

    def reply(k):
        return copy(1, k, replies.at[rows_of(peer(k)), :], mirrors.at[rows_of(me), :])

    each_peer(lambda k: reply(k).start())

    def block_at(b):
        return pl.ds(pl.multiple_of(b * groups, groups), groups)

    def edges_at(b):
        return pl.ds(pl.multiple_of(b * block, block), block)

    def from_masters(b, c):
        pick = pick_rows(sink_ref[block_at(b), :], 0, masters)
        picked[edges_at(b), :] = dot(pick, table[...], (1, 0)).astype(BF16)
        return c

    lax.fori_loop(0, blocks, from_masters, 0)

    each_peer(
        lambda k: to_low(2, k, partial.at[low_peer(k)], arrived.at[low_giver(k)]).wait_recv(), low
    )
    total = lax.fori_loop(
        1,
        low,
        lambda k, t: t + arrived[low_giver(k)].astype(F32),
        partial[at_low].astype(F32),
    ).astype(BF16)
    for c in range(owners):
        column_sum[c] = total[c * chunk : (c + 1) * chunk, :]

    def column_place():
        return lax.rem(at_high, owners)

    def scatter_high(k):
        return to_high(
            4, k, column_sum.at[lax.rem(high_peer(k), owners)], column_arrived.at[at_high]
        )

    each_peer(guarded(lambda k: scatter_high(k).start(), high_peer), high)

    each_peer(
        lambda k: copy(
            1, k, replies.at[rows_of(peer(k)), :], mirrors.at[rows_of(giver(k)), :]
        ).wait_recv()
    )
    mirror_sum[...] = jnp.zeros_like(mirror_sum)
    mirror_count = mirrors.shape[0]

    def from_mirrors(b, c):
        pick = pick_rows(sink_ref[block_at(b), :], masters, mirror_count)
        more = dot(pick, mirrors[...], (1, 0)).astype(BF16)
        row = picked[edges_at(b), :] + more
        picked[edges_at(b), :] = row
        return c

    lax.fori_loop(0, blocks, from_mirrors, 0)

    def column_spread(k):
        return to_high(5, k, column_total.at[column_place()], column_total.at[column_place()])

    def reduce_column():
        each_peer(
            lambda k: to_high(
                4,
                k,
                column_sum.at[lax.rem(high_peer(k), owners)],
                column_arrived.at[high_giver(k)],
            ).wait_recv(),
            high,
        )
        column_total[column_place()] = lax.fori_loop(
            1,
            high,
            lambda k, t: t + column_arrived[high_giver(k)].astype(F32),
            column_sum[column_place()].astype(F32),
        ).astype(BF16)
        each_peer(lambda k: column_spread(k).start(), high)

    if_owner(reduce_column)

    def to_mirrors(b, c):
        put = put_rows(live[block_at(b), :], masters, mirror_count)
        mirror_sum[...] += dot(put, picked[edges_at(b), :], (1, 0))
        return c

    lax.fori_loop(0, blocks, to_mirrors, 0)
    returns[...] = mirror_sum[...].astype(BF16)
    returned[rows_of(me), :] = returns[rows_of(me), :]

    def give_back(k):
        return copy(3, k, returns.at[rows_of(peer(k)), :], returned.at[rows_of(me), :])

    each_peer(lambda k: give_back(k).start())

    each_peer(
        guarded(
            lambda k: to_high(
                5,
                k,
                column_total.at[column_place()],
                column_total.at[lax.rem(high_giver(k), owners)],
            ).wait_recv(),
            high_giver,
        ),
        high,
    )
    full[at_low] = column_total[...]

    def spread(k):
        return to_low(6, k, column_total, full.at[at_low])

    each_peer(lambda k: spread(k).start(), low)

    loads[3].wait()
    master_sum[...] = dot(cols[0], w_self_ref[:, :width], (1, 1)) + dot(
        cols[1], w_self_ref[:, width:], (1, 1)
    )

    def to_masters(b, c):
        put = put_rows(live[block_at(b), :], 0, masters)
        master_sum[...] += dot(put, picked[edges_at(b), :], (1, 0))
        return c

    lax.fori_loop(0, blocks, to_masters, 0)

    each_peer(
        lambda k: copy(
            3, k, returns.at[rows_of(peer(k)), :], returned.at[rows_of(giver(k)), :]
        ).wait_recv()
    )
    hub_sum = lax.fori_loop(
        0,
        parts // batch,
        lambda i, t: t + dot(hits[i], returned[batch_at(i), :], (1, 0)),
        master_sum[:HUBS, :],
    )
    out_ref[:HUBS, :] = hub_sum.astype(BF16)
    out_ref[HUBS:, :] = master_sum[HUBS:, :].astype(BF16)

    each_peer(lambda k: to_low(6, k, column_total, full.at[low_giver(k)]).wait_recv(), low)
    weights_ref[...] = full[...]

    exchange.wait_send()
    each_peer(lambda k: request(k).wait_send())
    each_peer(lambda k: reply(k).wait_send())
    each_peer(lambda k: give_back(k).wait_send())
    each_peer(lambda k: scatter(k).wait_send(), low)
    each_peer(guarded(lambda k: scatter_high(k).wait_send(), high_peer), high)
    if_owner(lambda: each_peer(lambda k: column_spread(k).wait_send(), high))
    each_peer(lambda k: spread(k).wait_send(), low)


def ones_at(index, count, first):
    one, zero = jnp.ones((), BF16), jnp.zeros((), BF16)
    row = (lax.broadcasted_iota(jnp.int32, (count, LANES), 0) + first).astype(jnp.int16)
    index = index.astype(jnp.int16)
    return jnp.concatenate(
        [
            jnp.where(row == index[g : g + 1, :], one, zero).astype(F8)
            for g in range(index.shape[0])
        ],
        axis=1,
    )


def count_kernel(
    parts,
    low,
    block,
    limit_ref,
    grad_hbm,
    pre_hbm,
    features_hbm,
    mean_hbm,
    w_self_hbm,
    w_neigh_hbm,
    source_hbm,
    sink_hbm,
    wanted_hbm,
    degree_hbm,
    out_ref,
    weights_ref,
    grads,
    operands,
    w_self_ref,
    w_neigh_ref,
    edges,
    asking,
    degree_ref,
    wanted,
    cols,
    table,
    asked,
    replies,
    master_sum,
    returns,
    returned,
    hits,
    sinks,
    count_sum,
    counts,
    partial,
    arrived,
    column_sum,
    column_arrived,
    column_total,
    full,
    load_sems,
    feat_send,
    feat_recv,
    send_sems,
    recv_sems,
):
    me, half = lax.axis_index("dom"), lax.axis_index("feat")
    partner = 1 - half
    masters, width = out_ref.shape
    mirror_count = replies.shape[0]
    slots = mirror_count // parts
    mirrors = table.at[pl.ds(masters, mirror_count), :]
    rows = masters + mirror_count
    low_rows = partial.shape[2]
    high, chunk = column_sum.shape[1], column_sum.shape[2]
    at_high, at_low = me // low, lax.rem(me, low)
    groups = block // LANES
    blocks = sinks.shape[0]
    step = mirror_count // 2
    pieces = 2

    def chunk_at(i):
        return half if i == 0 else partner

    source_ref, sink_ref = edges.at[0], edges.at[1]

    def peer(k):
        return lax.rem(me + k, parts)

    def rows_of(q):
        return pl.ds(pl.multiple_of(q * slots, slots), slots)

    def half_at(h):
        return pl.ds(pl.multiple_of(h * width, width), width)

    def copy(stage, src, dst, device):
        return pltpu.make_async_remote_copy(
            src_ref=src,
            dst_ref=dst,
            send_sem=send_sems.at[stage],
            recv_sem=recv_sems.at[stage],
            device_id={"dom": device},
            device_id_type=MESH,
        )

    def all_of(stage, ref):
        return copy(stage, ref, ref, peer(1))

    def across(i, src, dst):
        return pltpu.make_async_remote_copy(
            src_ref=src,
            dst_ref=dst,
            send_sem=feat_send.at[i],
            recv_sem=feat_recv.at[i],
            device_id={"feat": partner},
            device_id_type=MESH,
        )

    def each_peer(act, count=parts):
        lax.fori_loop(1, count, lambda k, c: (act(k), c)[1], 0)

    def load(i, *pairs):
        for src, dst in pairs:
            pltpu.make_async_copy(src, dst, load_sems.at[i]).start()

    def loaded(i, ref):
        pltpu.make_async_copy(ref, ref, load_sems.at[i]).wait()

    barrier = pltpu.get_barrier_semaphore()
    pl.semaphore_signal(barrier, inc=1, device_id={"feat": partner}, device_id_type=MESH)
    each_peer(
        lambda k: pl.semaphore_signal(
            barrier, inc=1, device_id={"dom": peer(k)}, device_id_type=MESH
        )
    )
    load(0, (grad_hbm, grads.at[0]), (pre_hbm, grads.at[1]))
    load(1, (features_hbm, operands.at[0]), (mean_hbm, operands.at[1]))
    load(2, (wanted_hbm, asking))
    load(3, (source_hbm, edges.at[0]), (sink_hbm, edges.at[1]))
    load(4, (w_neigh_hbm, w_neigh_ref))
    load(5, (degree_hbm, degree_ref))
    load(6, (w_self_hbm, w_self_ref))
    loaded(0, grads)
    keep = (grads[1] > 0).astype(F32)
    cols[half] = (grads[0].astype(F32) * keep).astype(BF16)

    per_weight = low // 2

    def weigh(h):
        for i in range(2):
            part = dot(operands[i], cols[h], (0, 0)).astype(BF16)
            for c in range(per_weight):
                partial[h, i * per_weight + c] = part[c * low_rows : (c + 1) * low_rows, :]

    def low_peer(k):
        return lax.rem(at_low + k, low)

    def low_giver(k):
        return lax.rem(at_low + (low - k), low)

    def high_peer(k):
        return lax.rem(at_high + k, high)

    def high_giver(k):
        return lax.rem(at_high + (high - k), high)

    def to_low(stage, k, src, dst):
        return copy(stage, src, dst, at_high * low + low_peer(k))

    def to_high(stage, k, src, dst):
        return copy(stage, src, dst, high_peer(k) * low + at_low)

    def scatter(i, k):
        h = chunk_at(i)
        return to_low(3 + i, k, partial.at[h, low_peer(k)], arrived.at[h, at_low])

    def scatter_high(i, k):
        h = chunk_at(i)
        return to_high(3 + pieces + i, k, column_sum.at[h, high_peer(k)], column_arrived.at[h, at_high])

    def spread_high(i, k):
        h = chunk_at(i)
        return to_high(3 + 2 * pieces + i, k, column_total.at[h, at_high], column_total.at[h, at_high])

    def spread(i, k):
        h = chunk_at(i)
        return to_low(3 + 3 * pieces + i, k, column_total.at[h], full.at[h, at_low])

    def low_batch(ref, i):
        return ref.at[chunk_at(i), pl.ds(0, low - 1)]

    def high_batch(ref, i):
        return ref.at[chunk_at(i), pl.ds(0, high - 1)]

    def add_low(i):
        h = chunk_at(i)
        all_of(3 + i, low_batch(arrived, i)).wait_recv()
        total = partial[h, at_low].astype(F32)
        for k in range(1, low):
            total = total + arrived[h, low_giver(k)].astype(F32)
        total = total.astype(BF16)
        for c in range(high):
            column_sum[h, c] = total[c * chunk : (c + 1) * chunk, :]
        each_peer(lambda k: scatter_high(i, k).start(), high)

    def add_high(i):
        h = chunk_at(i)
        all_of(3 + pieces + i, high_batch(column_arrived, i)).wait_recv()
        total = column_sum[h, at_high].astype(F32)
        for k in range(1, high):
            total = total + column_arrived[h, high_giver(k)].astype(F32)
        column_total[h, at_high] = total.astype(BF16)
        each_peer(lambda k: spread_high(i, k).start(), high)

    def pass_on(i):
        h = chunk_at(i)
        all_of(3 + 2 * pieces + i, high_batch(column_total, i)).wait_recv()
        each_peer(lambda k: spread(i, k).start(), low)
        full[h, at_low] = column_total[h]

    def finish(i):
        h = chunk_at(i)
        all_of(3 + 3 * pieces + i, low_batch(full, i)).wait_recv()
        weights_ref[h] = full[h]

    def block_at(b):
        return pl.ds(b * groups, groups)

    def lay_sinks(b):
        sinks[b] = ones_at(sink_ref[block_at(b), :], rows, 0)

    loaded(1, operands)
    weigh(half)
    loaded(2, asking)
    per_row = LANES // slots
    lane = lax.broadcasted_iota(jnp.int32, (1, LANES), 1) // slots == lax.rem(me, per_row)
    for p in range(parts):
        at = (p % per_row) * slots
        row = asking[p // per_row : p // per_row + 1, at : at + slots]
        wanted[p] = jnp.where(lane, jnp.concatenate([row] * per_row, axis=1), -1)
    asked[me] = wanted[me]
    loaded(3, edges)
    place = (
        lax.broadcasted_iota(jnp.int32, source_ref.shape, 0) * LANES
        + lax.broadcasted_iota(jnp.int32, source_ref.shape, 1)
    )
    source_ref[...] = jnp.where(place < limit_ref[0], source_ref[...], -1)
    pl.semaphore_wait(barrier, parts)

    hub_rows, other_rows = pl.ds(0, HUBS), pl.ds(HUBS, masters - HUBS)

    def exchange(i, h):
        at = (hub_rows, other_rows)[i]
        return across(i, cols.at[half, at, :], cols.at[h, at, :])

    exchange(0, half).start()

    def request(k):
        return copy(0, wanted.at[peer(k)], asked.at[me], peer(k))

    def reply(k):
        return copy(1, replies.at[rows_of(peer(k)), :], mirrors.at[rows_of(me), :], peer(k))

    def give_back(k):
        return copy(2, returns.at[rows_of(peer(k)), :], returned.at[rows_of(me), :], peer(k))

    others = pl.ds(0, (parts - 1) * slots)
    each_peer(lambda k: request(k).start())
    exchange(1, half).start()
    each_peer(lambda k: scatter(0, k).start(), low)
    loaded(4, w_neigh_ref)
    loaded(5, degree_ref)

    def scale(first, count):
        at = pl.ds(first, count)
        neigh = dot(cols[0, at, :], w_neigh_ref[:, :width], (1, 1)) + dot(
            cols[1, at, :], w_neigh_ref[:, width:], (1, 1)
        )
        for g in range(0, count, LANES):
            size = min(LANES, count - g)
            row = (first + g) // LANES
            degree = columns_of(degree_ref[row : row + 1, :])[:size, :].astype(F32)
            degree = jnp.concatenate([degree] * (width // LANES), axis=1)
            table[first + g : first + g + size, :] = (neigh[g : g + size, :] / degree).astype(BF16)

    exchange(0, partner).wait_recv()
    exchange(1, partner).wait_recv()
    weigh(partner)
    each_peer(lambda k: scatter(1, k).start(), low)
    scale(0, masters)
    all_of(0, asked.at[pl.ds(0, parts - 1)]).wait_recv()
    hub = lax.broadcasted_iota(jnp.int32, (HUBS, LANES), 0)
    for g in range(parts // per_row):
        row = asked[g * per_row]
        for p in range(1, per_row):
            row = jnp.maximum(row, asked[g * per_row + p])
        hits[:, g * LANES : (g + 1) * LANES] = jnp.where(
            hub == row, jnp.ones((), BF16), jnp.zeros((), BF16)
        )
    replies[...] = dot(hits[...], table[:HUBS, :], (0, 0)).astype(BF16)
    each_peer(lambda k: reply(k).start())
    mirrors[rows_of(me), :] = replies[rows_of(me), :]
    def count_at(r, h):
        first = masters + h * step if r == 0 else h * (masters // 2) + (r - 1) * step
        return pl.ds(pl.multiple_of(first, step), step)

    def count(r, b):
        first = masters + half * step if r == 0 else half * (masters // 2) + (r - 1) * step
        source = ones_at(source_ref[block_at(b), :], step, first)
        if r == 0:
            lay_sinks(b)
        if b < blocks - 1:
            term = dot(source, sinks[b], (1, 1))
            count_sum[...] = term if b == 0 else count_sum[...] + term
            return
        for c in range(2):
            at = slice(c * (rows // 2), (c + 1) * (rows // 2))
            term = dot(source, sinks[b, at, :], (1, 1)) + count_sum[:, at]
            counts[c, count_at(r, half), :] = term.astype(BF16)
            send_counts(r, c).start()

    def send_counts(r, c):
        mine = counts.at[c, count_at(r, half), :]
        return across(2 + 2 * r + c, mine, mine)

    def count_arrives(r):
        for c in range(2):
            other = counts.at[c, count_at(r, partner), :]
            across(2 + 2 * r + c, other, other).wait_recv()

    def return_mirrors():
        count_arrives(0)
        cut = rows // 2
        own_part = dot(counts[0, masters:, :], table[:cut, :], (1, 0)) + dot(
            counts[1, masters:, : masters - cut], table[cut:masters, :], (1, 0)
        )
        all_of(1, mirrors.at[others, :]).wait_recv()
        mirror_sum = own_part + dot(
            counts[1, masters:, masters - cut :], table[masters:, :], (1, 0)
        )
        returns[...] = mirror_sum.astype(BF16)
        each_peer(lambda k: give_back(k).start())
        returned[rows_of(me), :] = returns[rows_of(me), :]

    last = masters // mirror_count
    acts = {"ret": return_mirrors}
    for i in range(pieces):
        acts["al", i] = functools.partial(add_low, i)
        acts["ah", i] = functools.partial(add_high, i)
        acts["po", i] = functools.partial(pass_on, i)
    plan = {
        "early": (),
        0: (("al", 0),),
        1: (("al", 1),),
        2: (("ah", 0),),
        3: (("ah", 1), "ret",),
        4: (("po", 0), ("po", 1),),
        5: (),
        "mid": (),
        "late": (),
    }
    for a in plan["early"]:
        acts[a]()
    for unit in range((last + 1) * blocks):
        count(unit // blocks, unit % blocks)
        for a in plan.get(unit, ()):
            acts[a]()
    loaded(6, w_self_ref)

    def settle(h):
        at = pl.ds(pl.multiple_of(h * (masters // 2), masters // 2), masters // 2)
        total = (
            dot(cols[0, at, :], w_self_ref[:, :width], (1, 1))
            + dot(cols[1, at, :], w_self_ref[:, width:], (1, 1))
            + dot(counts[0, at, :], table[: rows // 2, :], (1, 0))
            + dot(counts[1, at, :], table[rows // 2 :, :], (1, 0))
        )
        master_sum[at, :] = total
        out_ref[at, :] = total.astype(BF16)

    settle(half)
    for a in plan["mid"]:
        acts[a]()
    for r in range(1, last + 1):
        count_arrives(r)
    settle(partner)
    for a in plan["late"]:
        acts[a]()
    all_of(2, returned.at[others, :]).wait_recv()
    hub_sum = master_sum[:HUBS, :] + dot(hits[...], returned[...], (1, 0))
    out_ref[:HUBS, :] = hub_sum.astype(BF16)
    for i in range(pieces):
        finish(i)

    exchange(0, half).wait_send()
    exchange(1, half).wait_send()
    for r in range(last + 1):
        for c in range(2):
            send_counts(r, c).wait_send()
    all_of(0, wanted.at[pl.ds(0, parts - 1)]).wait_send()
    all_of(1, replies.at[others, :]).wait_send()
    all_of(2, returns.at[others, :]).wait_send()
    for i in range(pieces):
        all_of(3 + i, low_batch(partial, i)).wait_send()
        all_of(3 + pieces + i, high_batch(column_sum, i)).wait_send()
        all_of(3 + 2 * pieces + i, high_batch(column_total, i)).wait_send()
        all_of(3 + 3 * pieces + i, low_batch(full, i)).wait_send()


def settle_kernel(grad_ref, weights_ref, out_ref, self_ref, neigh_ref):
    out_ref[...] = grad_ref[...]
    halves, low, high, chunk, width = weights_ref.shape
    rows = (low // 2) * high * chunk
    for w, ref in enumerate((self_ref, neigh_ref)):
        for h in range(halves):
            block = weights_ref[h, w * (low // 2) : (w + 1) * (low // 2)].reshape(rows, width)
            ref[:, h * width : (h + 1) * width] = block.astype(F32)


def on_device(
    features,
    grad_out,
    pre_act,
    neigh_mean,
    w_self,
    w_neigh,
    edge_from,
    edge_to,
    edge_count,
    mirror_master,
    degrees,
):
    masters, width = features.shape
    parts = lax.axis_size("dom")
    mirror_count = mirror_master.shape[0]
    slots = mirror_count // parts
    edges = edge_from.shape[0]
    full = w_self.shape[1]
    weight_rows = 2 * w_self.shape[0]
    low = 2
    while parts % (4 * low) == 0 and 4 * low * low <= parts:
        low *= 2
    low_rows = weight_rows // low
    owners = min(parts // low, low_rows // 16)
    chunk = low_rows // owners
    batch = 8 if parts % 8 == 0 else 1
    block = min(edges, 2048 if masters + mirror_count <= 2048 else 256)
    vmem = pl.BlockSpec(memory_space=pltpu.VMEM)
    anywhere = pl.BlockSpec(memory_space=pl.ANY)
    step = mirror_count // 2
    if (
        masters + mirror_count <= 2048
        and owners * low == parts
        and parts % (LANES // slots) == 0
        and masters % mirror_count == 0
        and edges % 4096 == 0
        and chunk % 16 == 0
    ):
        high = owners
        part = chunk
        count_block = edges // 2
        weight = jax.ShapeDtypeStruct(w_self.shape, F32)
        rows = masters + mirror_count
        sent = pl.pallas_call(
            functools.partial(count_kernel, parts, low, count_block),
            out_shape=(
                pltpu.VMEM((masters, width), BF16),
                pltpu.VMEM((2, low, high, part, width), BF16),
            ),
            in_specs=[pl.BlockSpec(memory_space=pltpu.SMEM)] + [anywhere] * 10,
            out_specs=(vmem, vmem),
            scratch_shapes=[
                pltpu.VMEM((2, masters, width), BF16),
                pltpu.VMEM((2, masters, width), BF16),
                pltpu.VMEM(w_self.shape, BF16),
                pltpu.VMEM(w_self.shape, BF16),
                pltpu.VMEM((2, edges // LANES, LANES), jnp.int32),
                pltpu.VMEM((mirror_count // LANES, LANES), jnp.int32),
                pltpu.VMEM((masters // LANES, LANES), jnp.int32),
                pltpu.VMEM((parts, 1, LANES), jnp.int32),
                pltpu.VMEM((2, masters, width), BF16),
                pltpu.VMEM((rows, width), BF16),
                pltpu.VMEM((parts, 1, LANES), jnp.int32),
                pltpu.VMEM((mirror_count, width), BF16),
                pltpu.VMEM((masters, width), F32),
                pltpu.VMEM((mirror_count, width), BF16),
                pltpu.VMEM((mirror_count, width), BF16),
                pltpu.VMEM((HUBS, mirror_count), BF16),
                pltpu.VMEM((edges // count_block, rows, count_block), F8),
                pltpu.VMEM((step, rows), F32),
                pltpu.VMEM((2, rows, rows // 2), BF16),
                pltpu.VMEM((2, low, high * part, width), BF16),
                pltpu.VMEM((2, low, high * part, width), BF16),
                pltpu.VMEM((2, high, part, width), BF16),
                pltpu.VMEM((2, high, part, width), BF16),
                pltpu.VMEM((2, high, part, width), BF16),
                pltpu.VMEM((2, low, high, part, width), BF16),
                pltpu.SemaphoreType.DMA((7,)),
                pltpu.SemaphoreType.DMA((4 + 2 * (masters // mirror_count),)),
                pltpu.SemaphoreType.DMA((4 + 2 * (masters // mirror_count),)),
                pltpu.SemaphoreType.DMA((11,)),
                pltpu.SemaphoreType.DMA((11,)),
            ],
            compiler_params=pltpu.CompilerParams(
                collective_id=1, has_side_effects=True, vmem_limit_bytes=54 * 2**20
            ),
        )(
            edge_count,
            grad_out,
            pre_act,
            features,
            neigh_mean,
            w_self,
            w_neigh,
            edge_from.reshape(-1, LANES),
            edge_to.reshape(-1, LANES),
            mirror_master.reshape(-1, LANES),
            degrees.reshape(-1, LANES),
        )
        return pl.pallas_call(
            settle_kernel,
            out_shape=(jax.ShapeDtypeStruct((masters, width), BF16), weight, weight),
            in_specs=[vmem] * 2,
            out_specs=(vmem,) * 3,
        )(*[pltpu.with_memory_space_constraint(x, pltpu.VMEM) for x in sent])
    input_grad, weights = pl.pallas_call(
        functools.partial(layer_kernel, parts, block),
        out_shape=(
            jax.ShapeDtypeStruct((masters, width), BF16),
            jax.ShapeDtypeStruct((low, owners, chunk, full), BF16),
        ),
        in_specs=[pl.BlockSpec(memory_space=pltpu.SMEM)] + [vmem] * 2 + [anywhere] * 4 + [vmem] * 4,
        out_specs=(vmem, vmem),
        scratch_shapes=[
            pltpu.VMEM(features.shape, BF16),
            pltpu.VMEM(features.shape, BF16),
            pltpu.VMEM(w_self.shape, BF16),
            pltpu.VMEM(w_self.shape, BF16),
            pltpu.VMEM((2, masters, width), BF16),
            pltpu.VMEM((edges // LANES, LANES), jnp.int32),
            pltpu.VMEM((masters, width), BF16),
            pltpu.VMEM((parts, 1, slots), jnp.int32),
            pltpu.VMEM((mirror_count, width), BF16),
            pltpu.VMEM((mirror_count, width), BF16),
            pltpu.VMEM((edges, width), BF16),
            pltpu.VMEM((masters, width), F32),
            pltpu.VMEM((mirror_count, width), F32),
            pltpu.VMEM((mirror_count, width), BF16),
            pltpu.VMEM((mirror_count, width), BF16),
            pltpu.VMEM((parts // batch, HUBS, batch * slots), BF16),
            pltpu.VMEM((low, low_rows, full), BF16),
            pltpu.VMEM((low, low_rows, full), BF16),
            pltpu.VMEM((owners, chunk, full), BF16),
            pltpu.VMEM((parts // low, chunk, full), BF16),
            pltpu.VMEM((owners, chunk, full), BF16),
            pltpu.VMEM((low, owners, chunk, full), BF16),
            pltpu.SemaphoreType.DMA((4,)),
            pltpu.SemaphoreType.DMA((2,)),
            pltpu.SemaphoreType.DMA((7, parts)),
            pltpu.SemaphoreType.DMA((7, parts)),
        ],
        compiler_params=pltpu.CompilerParams(
            collective_id=0, has_side_effects=True, vmem_limit_bytes=60 * 2**20
        ),
    )(
        edge_count,
        grad_out,
        pre_act,
        features,
        neigh_mean,
        w_self,
        w_neigh,
        edge_from.reshape(-1, LANES),
        edge_to.reshape(-1, LANES),
        mirror_master.reshape(parts, 1, slots),
        degrees.reshape(-1, LANES),
    )
    weights = weights.reshape(2, w_self.shape[0], full).astype(F32)
    return (input_grad, weights[0], weights[1])


def solution(mesh):
    placed = (
        P("dom", "feat"),
        P("dom", "feat"),
        P("dom", "feat"),
        P("dom", "feat"),
        P("feat", None),
        P("feat", None),
        P("dom"),
        P("dom"),
        P("dom"),
        P("dom"),
        P("dom"),
    )
    return jax.shard_map(
        on_device,
        mesh=mesh,
        in_specs=placed,
        out_specs=(P("dom", "feat"), P("feat", None), P("feat", None)),
        check_vma=False,
    )
```

```python
import functools

import jax
import jax.numpy as jnp
from jax import lax
from jax.experimental import pallas as pl
from jax.experimental.pallas import tpu as pltpu
from jax.sharding import PartitionSpec as P

LANES = 128
HUBS = 64
MESH = pl.DeviceIdType.MESH
F32, BF16, F8 = jnp.float32, jnp.bfloat16, jnp.float8_e4m3fn


def dot(a, b, over):
    return lax.dot_general(a, b, ((over[:1], over[1:]), ((), ())), preferred_element_type=F32)


def columns_of(row):
    return jnp.transpose(jnp.broadcast_to(row, (LANES, LANES)))


def pick_rows(sinks, first, count):
    one, zero = jnp.ones((), BF16), jnp.zeros((), BF16)
    lane = lax.broadcasted_iota(jnp.int32, (LANES, LANES), 1)
    tiles = []
    for g in range(sinks.shape[0]):
        column = columns_of(sinks[g : g + 1, :])
        tiles.append(
            jnp.concatenate(
                [jnp.where(column == lane + (first + j), one, zero) for j in range(0, count, LANES)],
                axis=1,
            )
        )
    return jnp.concatenate(tiles, axis=0)


def put_rows(sources, first, count):
    one, zero = jnp.ones((), BF16), jnp.zeros((), BF16)
    row = lax.broadcasted_iota(jnp.int32, (count, LANES), 0) + first
    return jnp.concatenate(
        [jnp.where(row == sources[g : g + 1, :], one, zero) for g in range(sources.shape[0])],
        axis=1,
    )


def layer_kernel(
    parts,
    block,
    limit_ref,
    grad_ref,
    pre_ref,
    features_hbm,
    mean_hbm,
    w_self_hbm,
    w_neigh_hbm,
    source_ref,
    sink_ref,
    wanted_ref,
    degree_ref,
    out_ref,
    weights_ref,
    features_ref,
    mean_ref,
    w_self_ref,
    w_neigh_ref,
    cols,
    live,
    table,
    asked,
    replies,
    mirrors,
    picked,
    master_sum,
    mirror_sum,
    returns,
    returned,
    hits,
    partial,
    arrived,
    column_sum,
    column_arrived,
    column_total,
    full,
    load_sems,
    feat_sems,
    send_sems,
    recv_sems,
):
    me, half = lax.axis_index("dom"), lax.axis_index("feat")
    partner = 1 - half
    masters, width = grad_ref.shape
    slots = wanted_ref.shape[2]
    low, low_rows = partial.shape[0], partial.shape[1]
    owners, chunk = column_sum.shape[0], column_sum.shape[1]
    high = parts // low
    at_high, at_low = me // low, lax.rem(me, low)
    groups = block // LANES
    blocks = sink_ref.shape[0] // groups

    def peer(k):
        return lax.rem(me + k, parts)

    def giver(k):
        return lax.rem(me + (parts - k), parts)

    def rows_of(q):
        return pl.ds(pl.multiple_of(q * slots, slots), slots)

    def copy(stage, k, src, dst, device=None):
        return pltpu.make_async_remote_copy(
            src_ref=src,
            dst_ref=dst,
            send_sem=send_sems.at[stage, k],
            recv_sem=recv_sems.at[stage, k],
            device_id={"dom": peer(k) if device is None else device},
            device_id_type=MESH,
        )

    def each_peer(act, count=parts):
        lax.fori_loop(1, count, lambda k, c: (act(k), c)[1], 0)

    loads = [
        pltpu.make_async_copy(src, dst, load_sems.at[i])
        for i, (src, dst) in enumerate(
            (
                (w_neigh_hbm, w_neigh_ref),
                (features_hbm, features_ref),
                (mean_hbm, mean_ref),
                (w_self_hbm, w_self_ref),
            )
        )
    ]

    barrier = pltpu.get_barrier_semaphore()
    pl.semaphore_signal(barrier, inc=1, device_id={"feat": partner}, device_id_type=MESH)
    each_peer(
        lambda k: pl.semaphore_signal(
            barrier, inc=1, device_id={"dom": peer(k)}, device_id_type=MESH
        )
    )
    for load in loads:
        load.start()
    keep = (pre_ref[...] > 0).astype(F32)
    cols[half] = (grad_ref[...].astype(F32) * keep).astype(BF16)
    place = (
        lax.broadcasted_iota(jnp.int32, source_ref.shape, 0) * LANES
        + lax.broadcasted_iota(jnp.int32, source_ref.shape, 1)
    )
    live[...] = jnp.where(place < limit_ref[0], source_ref[...], -1)
    asked[me] = wanted_ref[me]
    pl.semaphore_wait(barrier, parts)

    exchange = pltpu.make_async_remote_copy(
        src_ref=cols.at[half],
        dst_ref=cols.at[half],
        send_sem=feat_sems.at[0],
        recv_sem=feat_sems.at[1],
        device_id={"feat": partner},
        device_id_type=MESH,
    )
    exchange.start()

    def request(k):
        return copy(0, k, wanted_ref.at[peer(k)], asked.at[me])

    each_peer(lambda k: request(k).start())
    def half_at(h):
        return pl.ds(pl.multiple_of(h * width, width), width)

    loads[0].wait()
    own = dot(cols[half], w_neigh_ref[:, half_at(half)], (1, 1))
    pltpu.make_async_remote_copy(
        src_ref=cols.at[half],
        dst_ref=cols.at[partner],
        send_sem=feat_sems.at[0],
        recv_sem=feat_sems.at[1],
        device_id={"feat": partner},
        device_id_type=MESH,
    ).wait_recv()

    both = jnp.concatenate([cols[0], cols[1]], axis=1)
    per_weight = low // 2
    for i, operand in enumerate((features_ref, mean_ref)):
        loads[1 + i].wait()
        part = dot(operand[...], both, (0, 0)).astype(BF16)
        for c in range(per_weight):
            partial[i * per_weight + c] = part[c * low_rows : (c + 1) * low_rows, :]

    def low_peer(k):
        return lax.rem(at_low + k, low)

    def low_giver(k):
        return lax.rem(at_low + (low - k), low)

    def high_peer(k):
        return lax.rem(at_high + k, high)

    def high_giver(k):
        return lax.rem(at_high + (high - k), high)

    def to_low(stage, k, src, dst):
        return copy(stage, k, src, dst, at_high * low + low_peer(k))

    def to_high(stage, k, src, dst):
        return copy(stage, k, src, dst, high_peer(k) * low + at_low)

    def guarded(act, owner):
        if owners == high:
            return act
        return lambda k: pl.when(owner(k) < owners)(lambda: act(k))

    def if_owner(act):
        if owners == high:
            act()
        else:
            pl.when(at_high < owners)(act)

    def scatter(k):
        return to_low(2, k, partial.at[low_peer(k)], arrived.at[at_low])

    each_peer(lambda k: scatter(k).start(), low)
    neigh = own + dot(cols[partner], w_neigh_ref[:, half_at(partner)], (1, 1))
    for g in range(masters // LANES):
        at = slice(g * LANES, (g + 1) * LANES)
        degree = columns_of(degree_ref[g : g + 1, :]).astype(F32)
        degree = jnp.concatenate([degree] * (width // LANES), axis=1)
        table[at, :] = (neigh[at, :] / degree).astype(BF16)

    each_peer(lambda k: copy(0, k, wanted_ref.at[peer(k)], asked.at[giver(k)]).wait_recv())

    batch = 8 if parts % 8 == 0 else 1
    hub = lax.broadcasted_iota(jnp.int32, (HUBS, slots), 0)

    def batch_at(i):
        return pl.ds(pl.multiple_of(i * batch * slots, batch * slots), batch * slots)

    def answer(i, c):
        hit = jnp.concatenate(
            [
                jnp.where(hub == asked[i * batch + j], jnp.ones((), BF16), jnp.zeros((), BF16))
                for j in range(batch)
            ],
            axis=1,
        )
        hits[i] = hit
        replies[batch_at(i), :] = dot(hit, table[:HUBS, :], (0, 0)).astype(BF16)
        return c

    lax.fori_loop(0, parts // batch, answer, 0)
    mirrors[rows_of(me), :] = replies[rows_of(me), :]

    def reply(k):
        return copy(1, k, replies.at[rows_of(peer(k)), :], mirrors.at[rows_of(me), :])

    each_peer(lambda k: reply(k).start())

    def block_at(b):
        return pl.ds(pl.multiple_of(b * groups, groups), groups)

    def edges_at(b):
        return pl.ds(pl.multiple_of(b * block, block), block)

    def from_masters(b, c):
        pick = pick_rows(sink_ref[block_at(b), :], 0, masters)
        picked[edges_at(b), :] = dot(pick, table[...], (1, 0)).astype(BF16)
        return c

    lax.fori_loop(0, blocks, from_masters, 0)

    each_peer(
        lambda k: to_low(2, k, partial.at[low_peer(k)], arrived.at[low_giver(k)]).wait_recv(), low
    )
    total = lax.fori_loop(
        1,
        low,
        lambda k, t: t + arrived[low_giver(k)].astype(F32),
        partial[at_low].astype(F32),
    ).astype(BF16)
    for c in range(owners):
        column_sum[c] = total[c * chunk : (c + 1) * chunk, :]

    def column_place():
        return lax.rem(at_high, owners)

    def scatter_high(k):
        return to_high(
            4, k, column_sum.at[lax.rem(high_peer(k), owners)], column_arrived.at[at_high]
        )

    each_peer(guarded(lambda k: scatter_high(k).start(), high_peer), high)

    each_peer(
        lambda k: copy(
            1, k, replies.at[rows_of(peer(k)), :], mirrors.at[rows_of(giver(k)), :]
        ).wait_recv()
    )
    mirror_sum[...] = jnp.zeros_like(mirror_sum)
    mirror_count = mirrors.shape[0]

    def from_mirrors(b, c):
        pick = pick_rows(sink_ref[block_at(b), :], masters, mirror_count)
        more = dot(pick, mirrors[...], (1, 0)).astype(BF16)
        row = picked[edges_at(b), :] + more
        picked[edges_at(b), :] = row
        return c

    lax.fori_loop(0, blocks, from_mirrors, 0)

    def column_spread(k):
        return to_high(5, k, column_total.at[column_place()], column_total.at[column_place()])

    def reduce_column():
        each_peer(
            lambda k: to_high(
                4,
                k,
                column_sum.at[lax.rem(high_peer(k), owners)],
                column_arrived.at[high_giver(k)],
            ).wait_recv(),
            high,
        )
        column_total[column_place()] = lax.fori_loop(
            1,
            high,
            lambda k, t: t + column_arrived[high_giver(k)].astype(F32),
            column_sum[column_place()].astype(F32),
        ).astype(BF16)
        each_peer(lambda k: column_spread(k).start(), high)

    if_owner(reduce_column)

    def to_mirrors(b, c):
        put = put_rows(live[block_at(b), :], masters, mirror_count)
        mirror_sum[...] += dot(put, picked[edges_at(b), :], (1, 0))
        return c

    lax.fori_loop(0, blocks, to_mirrors, 0)
    returns[...] = mirror_sum[...].astype(BF16)
    returned[rows_of(me), :] = returns[rows_of(me), :]

    def give_back(k):
        return copy(3, k, returns.at[rows_of(peer(k)), :], returned.at[rows_of(me), :])

    each_peer(lambda k: give_back(k).start())

    each_peer(
        guarded(
            lambda k: to_high(
                5,
                k,
                column_total.at[column_place()],
                column_total.at[lax.rem(high_giver(k), owners)],
            ).wait_recv(),
            high_giver,
        ),
        high,
    )
    full[at_low] = column_total[...]

    def spread(k):
        return to_low(6, k, column_total, full.at[at_low])

    each_peer(lambda k: spread(k).start(), low)

    loads[3].wait()
    master_sum[...] = dot(cols[0], w_self_ref[:, :width], (1, 1)) + dot(
        cols[1], w_self_ref[:, width:], (1, 1)
    )

    def to_masters(b, c):
        put = put_rows(live[block_at(b), :], 0, masters)
        master_sum[...] += dot(put, picked[edges_at(b), :], (1, 0))
        return c

    lax.fori_loop(0, blocks, to_masters, 0)

    each_peer(
        lambda k: copy(
            3, k, returns.at[rows_of(peer(k)), :], returned.at[rows_of(giver(k)), :]
        ).wait_recv()
    )
    hub_sum = lax.fori_loop(
        0,
        parts // batch,
        lambda i, t: t + dot(hits[i], returned[batch_at(i), :], (1, 0)),
        master_sum[:HUBS, :],
    )
    out_ref[:HUBS, :] = hub_sum.astype(BF16)
    out_ref[HUBS:, :] = master_sum[HUBS:, :].astype(BF16)

    each_peer(lambda k: to_low(6, k, column_total, full.at[low_giver(k)]).wait_recv(), low)
    weights_ref[...] = full[...]

    exchange.wait_send()
    each_peer(lambda k: request(k).wait_send())
    each_peer(lambda k: reply(k).wait_send())
    each_peer(lambda k: give_back(k).wait_send())
    each_peer(lambda k: scatter(k).wait_send(), low)
    each_peer(guarded(lambda k: scatter_high(k).wait_send(), high_peer), high)
    if_owner(lambda: each_peer(lambda k: column_spread(k).wait_send(), high))
    each_peer(lambda k: spread(k).wait_send(), low)


def ones_at(index, count, first):
    one, zero = jnp.ones((), BF16), jnp.zeros((), BF16)
    row = (lax.broadcasted_iota(jnp.int32, (count, LANES), 0) + first).astype(jnp.int16)
    index = index.astype(jnp.int16)
    return jnp.concatenate(
        [
            jnp.where(row == index[g : g + 1, :], one, zero).astype(F8)
            for g in range(index.shape[0])
        ],
        axis=1,
    )


def count_kernel(
    parts,
    low,
    block,
    limit_ref,
    grad_hbm,
    pre_hbm,
    features_hbm,
    mean_hbm,
    w_self_hbm,
    w_neigh_hbm,
    source_hbm,
    sink_hbm,
    wanted_hbm,
    degree_hbm,
    out_ref,
    weights_ref,
    grads,
    operands,
    w_self_ref,
    w_neigh_ref,
    edges,
    asking,
    degree_ref,
    wanted,
    cols,
    table,
    asked,
    replies,
    master_sum,
    returns,
    returned,
    hits,
    sinks,
    sources,
    count_sum,
    counts,
    partial,
    arrived,
    column_sum,
    column_arrived,
    column_total,
    full,
    load_sems,
    feat_send,
    feat_recv,
    send_sems,
    recv_sems,
):
    me, half = lax.axis_index("dom"), lax.axis_index("feat")
    partner = 1 - half
    masters, width = out_ref.shape
    mirror_count = replies.shape[0]
    slots = mirror_count // parts
    mirrors = table.at[pl.ds(masters, mirror_count), :]
    rows = masters + mirror_count
    low_rows = partial.shape[2]
    high, chunk = column_sum.shape[1], column_sum.shape[2]
    at_high, at_low = me // low, lax.rem(me, low)
    groups = block // LANES
    blocks = sinks.shape[0]
    step = mirror_count // 2
    pieces = 2

    def chunk_at(i):
        return half if i == 0 else partner

    source_ref, sink_ref = edges.at[0], edges.at[1]

    def peer(k):
        return lax.rem(me + k, parts)

    def rows_of(q):
        return pl.ds(pl.multiple_of(q * slots, slots), slots)

    def half_at(h):
        return pl.ds(pl.multiple_of(h * width, width), width)

    def copy(stage, src, dst, device):
        return pltpu.make_async_remote_copy(
            src_ref=src,
            dst_ref=dst,
            send_sem=send_sems.at[stage],
            recv_sem=recv_sems.at[stage],
            device_id={"dom": device},
            device_id_type=MESH,
        )

    def all_of(stage, ref):
        return copy(stage, ref, ref, peer(1))

    def across(i, src, dst):
        return pltpu.make_async_remote_copy(
            src_ref=src,
            dst_ref=dst,
            send_sem=feat_send.at[i],
            recv_sem=feat_recv.at[i],
            device_id={"feat": partner},
            device_id_type=MESH,
        )

    def each_peer(act, count=parts):
        lax.fori_loop(1, count, lambda k, c: (act(k), c)[1], 0)

    def load(i, *pairs):
        for src, dst in pairs:
            pltpu.make_async_copy(src, dst, load_sems.at[i]).start()

    def loaded(i, ref):
        pltpu.make_async_copy(ref, ref, load_sems.at[i]).wait()

    barrier = pltpu.get_barrier_semaphore()
    pl.semaphore_signal(barrier, inc=1, device_id={"feat": partner}, device_id_type=MESH)
    each_peer(
        lambda k: pl.semaphore_signal(
            barrier, inc=1, device_id={"dom": peer(k)}, device_id_type=MESH
        )
    )
    load(0, (grad_hbm, grads.at[0]), (pre_hbm, grads.at[1]))
    load(1, (features_hbm, operands.at[0]), (mean_hbm, operands.at[1]))
    load(2, (wanted_hbm, asking))
    load(3, (source_hbm, edges.at[0]), (sink_hbm, edges.at[1]))
    load(4, (w_neigh_hbm, w_neigh_ref))
    load(5, (degree_hbm, degree_ref))
    load(6, (w_self_hbm, w_self_ref))
    loaded(0, grads)
    keep = (grads[1] > 0).astype(F32)
    cols[half] = (grads[0].astype(F32) * keep).astype(BF16)

    per_weight = low // 2

    def weigh(h):
        for i in range(2):
            part = dot(operands[i], cols[h], (0, 0)).astype(BF16)
            for c in range(per_weight):
                partial[h, i * per_weight + c] = part[c * low_rows : (c + 1) * low_rows, :]

    def low_peer(k):
        return lax.rem(at_low + k, low)

    def low_giver(k):
        return lax.rem(at_low + (low - k), low)

    def high_peer(k):
        return lax.rem(at_high + k, high)

    def high_giver(k):
        return lax.rem(at_high + (high - k), high)

    def to_low(stage, k, src, dst):
        return copy(stage, src, dst, at_high * low + low_peer(k))

    def to_high(stage, k, src, dst):
        return copy(stage, src, dst, high_peer(k) * low + at_low)

    def scatter(i, k):
        h = chunk_at(i)
        return to_low(3 + i, k, partial.at[h, low_peer(k)], arrived.at[h, at_low])

    def scatter_high(i, k):
        h = chunk_at(i)
        return to_high(3 + pieces + i, k, column_sum.at[h, high_peer(k)], column_arrived.at[h, at_high])

    def spread_high(i, k):
        h = chunk_at(i)
        return to_high(3 + 2 * pieces + i, k, column_total.at[h, at_high], column_total.at[h, at_high])

    def spread(i, k):
        h = chunk_at(i)
        return to_low(3 + 3 * pieces + i, k, column_total.at[h], full.at[h, at_low])

    def low_batch(ref, i):
        return ref.at[chunk_at(i), pl.ds(0, low - 1)]

    def high_batch(ref, i):
        return ref.at[chunk_at(i), pl.ds(0, high - 1)]

    def add_low(i):
        h = chunk_at(i)
        all_of(3 + i, low_batch(arrived, i)).wait_recv()
        total = partial[h, at_low].astype(F32)
        for k in range(1, low):
            total = total + arrived[h, low_giver(k)].astype(F32)
        total = total.astype(BF16)
        for c in range(high):
            column_sum[h, c] = total[c * chunk : (c + 1) * chunk, :]
        each_peer(lambda k: scatter_high(i, k).start(), high)

    def add_high(i):
        h = chunk_at(i)
        all_of(3 + pieces + i, high_batch(column_arrived, i)).wait_recv()
        total = column_sum[h, at_high].astype(F32)
        for k in range(1, high):
            total = total + column_arrived[h, high_giver(k)].astype(F32)
        column_total[h, at_high] = total.astype(BF16)
        each_peer(lambda k: spread_high(i, k).start(), high)

    def pass_on(i):
        h = chunk_at(i)
        all_of(3 + 2 * pieces + i, high_batch(column_total, i)).wait_recv()
        each_peer(lambda k: spread(i, k).start(), low)
        full[h, at_low] = column_total[h]

    def finish(i):
        h = chunk_at(i)
        all_of(3 + 3 * pieces + i, low_batch(full, i)).wait_recv()
        weights_ref[h] = full[h]

    loaded(1, operands)
    weigh(half)
    loaded(2, asking)
    per_row = LANES // slots
    lane = lax.broadcasted_iota(jnp.int32, (1, LANES), 1) // slots == lax.rem(me, per_row)
    for p in range(parts):
        at = (p % per_row) * slots
        row = asking[p // per_row : p // per_row + 1, at : at + slots]
        wanted[p] = jnp.where(lane, jnp.concatenate([row] * per_row, axis=1), -1)
    asked[me] = wanted[me]
    loaded(3, edges)
    place = (
        lax.broadcasted_iota(jnp.int32, source_ref.shape, 0) * LANES
        + lax.broadcasted_iota(jnp.int32, source_ref.shape, 1)
    )
    source_ref[...] = jnp.where(place < limit_ref[0], source_ref[...], -1)
    pl.semaphore_wait(barrier, parts)

    hub_rows, other_rows = pl.ds(0, HUBS), pl.ds(HUBS, masters - HUBS)

    def exchange(i, h):
        at = (hub_rows, other_rows)[i]
        return across(i, cols.at[half, at, :], cols.at[h, at, :])

    exchange(0, half).start()

    def request(k):
        return copy(0, wanted.at[peer(k)], asked.at[me], peer(k))

    def reply(k):
        return copy(1, replies.at[rows_of(peer(k)), :], mirrors.at[rows_of(me), :], peer(k))

    def give_back(k):
        return copy(2, returns.at[rows_of(peer(k)), :], returned.at[rows_of(me), :], peer(k))

    others = pl.ds(0, (parts - 1) * slots)
    each_peer(lambda k: request(k).start())
    exchange(1, half).start()
    each_peer(lambda k: scatter(0, k).start(), low)
    loaded(4, w_neigh_ref)
    loaded(5, degree_ref)

    def scale(first, count):
        at = pl.ds(first, count)
        neigh = dot(cols[0, at, :], w_neigh_ref[:, :width], (1, 1)) + dot(
            cols[1, at, :], w_neigh_ref[:, width:], (1, 1)
        )
        for g in range(0, count, LANES):
            size = min(LANES, count - g)
            row = (first + g) // LANES
            degree = columns_of(degree_ref[row : row + 1, :])[:size, :].astype(F32)
            degree = jnp.concatenate([degree] * (width // LANES), axis=1)
            table[first + g : first + g + size, :] = (neigh[g : g + size, :] / degree).astype(BF16)

    def count_at(r, h):
        first = masters + h * step if r == 0 else h * (masters // 2) + (r - 1) * step
        return pl.ds(pl.multiple_of(first, step), step)

    def block_at(b):
        return pl.ds(b * groups, groups)

    def count(unit):
        r, c, b = unit // (2 * blocks), unit // blocks % 2, unit % blocks
        at = slice(c * (rows // 2), (c + 1) * (rows // 2))
        if r == 0:
            sinks[b, at, :] = ones_at(sink_ref[block_at(b), :], rows // 2, c * (rows // 2))
        if c == 0:
            first = masters + half * step if r == 0 else half * (masters // 2) + (r - 1) * step
            sources[b] = ones_at(source_ref[block_at(b), :], step, first)
        term = dot(sources[b], sinks[b, at, :], (1, 1))
        if b > 0:
            term = count_sum[...] + term
        if b < blocks - 1:
            count_sum[...] = term
            return
        counts[c, count_at(r, half), :] = term.astype(BF16)
        send_counts(r, c).start()

    def send_counts(r, c):
        mine = counts.at[c, count_at(r, half), :]
        return across(2 + 2 * r + c, mine, mine)

    count(0)
    count(1)
    exchange(0, partner).wait_recv()
    exchange(1, partner).wait_recv()
    weigh(partner)
    each_peer(lambda k: scatter(1, k).start(), low)
    scale(0, masters)
    all_of(0, asked.at[pl.ds(0, parts - 1)]).wait_recv()
    hub = lax.broadcasted_iota(jnp.int32, (HUBS, LANES), 0)
    for g in range(parts // per_row):
        row = asked[g * per_row]
        for p in range(1, per_row):
            row = jnp.maximum(row, asked[g * per_row + p])
        hits[:, g * LANES : (g + 1) * LANES] = jnp.where(
            hub == row, jnp.ones((), BF16), jnp.zeros((), BF16)
        )
    replies[...] = dot(hits[...], table[:HUBS, :], (0, 0)).astype(BF16)
    each_peer(lambda k: reply(k).start())
    mirrors[rows_of(me), :] = replies[rows_of(me), :]
    def count_arrives(r):
        for c in range(2):
            other = counts.at[c, count_at(r, partner), :]
            across(2 + 2 * r + c, other, other).wait_recv()

    def return_mirrors():
        count_arrives(0)
        cut = rows // 2
        own_part = dot(counts[0, masters:, :], table[:cut, :], (1, 0)) + dot(
            counts[1, masters:, : masters - cut], table[cut:masters, :], (1, 0)
        )
        all_of(1, mirrors.at[others, :]).wait_recv()
        mirror_sum = own_part + dot(
            counts[1, masters:, masters - cut :], table[masters:, :], (1, 0)
        )
        returns[...] = mirror_sum.astype(BF16)
        each_peer(lambda k: give_back(k).start())
        returned[rows_of(me), :] = returns[rows_of(me), :]

    last = masters // mirror_count
    acts = {"ret": return_mirrors}
    for i in range(pieces):
        acts["al", i] = functools.partial(add_low, i)
        acts["ah", i] = functools.partial(add_high, i)
        acts["po", i] = functools.partial(pass_on, i)
    plan = {
        "early": (),
        0: (),
        1: (),
        2: (("al", 0),),
        3: (),
        4: (),
        5: (("al", 1),),
        6: (),
        7: (("ah", 0),),
        8: (("ah", 1), "ret",),
        9: (("po", 0),),
        10: (),
        11: (("po", 1),),
        "mid": (),
        "late": (),
    }
    for a in plan["early"]:
        acts[a]()
    for unit in range(2, 2 * (last + 1) * blocks):
        count(unit)
        for a in plan.get(unit, ()):
            acts[a]()
    loaded(6, w_self_ref)

    def settle(h):
        at = pl.ds(pl.multiple_of(h * (masters // 2), masters // 2), masters // 2)
        total = (
            dot(cols[0, at, :], w_self_ref[:, :width], (1, 1))
            + dot(cols[1, at, :], w_self_ref[:, width:], (1, 1))
            + dot(counts[0, at, :], table[: rows // 2, :], (1, 0))
            + dot(counts[1, at, :], table[rows // 2 :, :], (1, 0))
        )
        master_sum[at, :] = total
        out_ref[at, :] = total.astype(BF16)

    settle(half)
    for a in plan["mid"]:
        acts[a]()
    for r in range(1, last + 1):
        count_arrives(r)
    settle(partner)
    for a in plan["late"]:
        acts[a]()
    all_of(2, returned.at[others, :]).wait_recv()
    hub_sum = master_sum[:HUBS, :] + dot(hits[...], returned[...], (1, 0))
    out_ref[:HUBS, :] = hub_sum.astype(BF16)
    for i in range(pieces):
        finish(i)

    exchange(0, half).wait_send()
    exchange(1, half).wait_send()
    for r in range(last + 1):
        for c in range(2):
            send_counts(r, c).wait_send()
    all_of(0, wanted.at[pl.ds(0, parts - 1)]).wait_send()
    all_of(1, replies.at[others, :]).wait_send()
    all_of(2, returns.at[others, :]).wait_send()
    for i in range(pieces):
        all_of(3 + i, low_batch(partial, i)).wait_send()
        all_of(3 + pieces + i, high_batch(column_sum, i)).wait_send()
        all_of(3 + 2 * pieces + i, high_batch(column_total, i)).wait_send()
        all_of(3 + 3 * pieces + i, low_batch(full, i)).wait_send()


def settle_kernel(grad_ref, weights_ref, out_ref, self_ref, neigh_ref):
    out_ref[...] = grad_ref[...]
    halves, low, high, chunk, width = weights_ref.shape
    rows = (low // 2) * high * chunk
    for w, ref in enumerate((self_ref, neigh_ref)):
        for h in range(halves):
            block = weights_ref[h, w * (low // 2) : (w + 1) * (low // 2)].reshape(rows, width)
            ref[:, h * width : (h + 1) * width] = block.astype(F32)


def on_device(
    features,
    grad_out,
    pre_act,
    neigh_mean,
    w_self,
    w_neigh,
    edge_from,
    edge_to,
    edge_count,
    mirror_master,
    degrees,
):
    masters, width = features.shape
    parts = lax.axis_size("dom")
    mirror_count = mirror_master.shape[0]
    slots = mirror_count // parts
    edges = edge_from.shape[0]
    full = w_self.shape[1]
    weight_rows = 2 * w_self.shape[0]
    low = 2
    while parts % (4 * low) == 0 and 4 * low * low <= parts:
        low *= 2
    low_rows = weight_rows // low
    owners = min(parts // low, low_rows // 16)
    chunk = low_rows // owners
    batch = 8 if parts % 8 == 0 else 1
    block = min(edges, 2048 if masters + mirror_count <= 2048 else 256)
    vmem = pl.BlockSpec(memory_space=pltpu.VMEM)
    anywhere = pl.BlockSpec(memory_space=pl.ANY)
    step = mirror_count // 2
    if (
        masters + mirror_count <= 2048
        and owners * low == parts
        and parts % (LANES // slots) == 0
        and masters % mirror_count == 0
        and edges % 4096 == 0
        and chunk % 16 == 0
    ):
        high = owners
        part = chunk
        count_block = edges // 2
        weight = jax.ShapeDtypeStruct(w_self.shape, F32)
        rows = masters + mirror_count
        sent = pl.pallas_call(
            functools.partial(count_kernel, parts, low, count_block),
            out_shape=(
                pltpu.VMEM((masters, width), BF16),
                pltpu.VMEM((2, low, high, part, width), BF16),
            ),
            in_specs=[pl.BlockSpec(memory_space=pltpu.SMEM)] + [anywhere] * 10,
            out_specs=(vmem, vmem),
            scratch_shapes=[
                pltpu.VMEM((2, masters, width), BF16),
                pltpu.VMEM((2, masters, width), BF16),
                pltpu.VMEM(w_self.shape, BF16),
                pltpu.VMEM(w_self.shape, BF16),
                pltpu.VMEM((2, edges // LANES, LANES), jnp.int32),
                pltpu.VMEM((mirror_count // LANES, LANES), jnp.int32),
                pltpu.VMEM((masters // LANES, LANES), jnp.int32),
                pltpu.VMEM((parts, 1, LANES), jnp.int32),
                pltpu.VMEM((2, masters, width), BF16),
                pltpu.VMEM((rows, width), BF16),
                pltpu.VMEM((parts, 1, LANES), jnp.int32),
                pltpu.VMEM((mirror_count, width), BF16),
                pltpu.VMEM((masters, width), F32),
                pltpu.VMEM((mirror_count, width), BF16),
                pltpu.VMEM((mirror_count, width), BF16),
                pltpu.VMEM((HUBS, mirror_count), BF16),
                pltpu.VMEM((edges // count_block, rows, count_block), F8),
                pltpu.VMEM((edges // count_block, step, count_block), F8),
                pltpu.VMEM((step, rows // 2), F32),
                pltpu.VMEM((2, rows, rows // 2), BF16),
                pltpu.VMEM((2, low, high * part, width), BF16),
                pltpu.VMEM((2, low, high * part, width), BF16),
                pltpu.VMEM((2, high, part, width), BF16),
                pltpu.VMEM((2, high, part, width), BF16),
                pltpu.VMEM((2, high, part, width), BF16),
                pltpu.VMEM((2, low, high, part, width), BF16),
                pltpu.SemaphoreType.DMA((7,)),
                pltpu.SemaphoreType.DMA((4 + 2 * (masters // mirror_count),)),
                pltpu.SemaphoreType.DMA((4 + 2 * (masters // mirror_count),)),
                pltpu.SemaphoreType.DMA((11,)),
                pltpu.SemaphoreType.DMA((11,)),
            ],
            compiler_params=pltpu.CompilerParams(
                collective_id=1, has_side_effects=True, vmem_limit_bytes=54 * 2**20
            ),
        )(
            edge_count,
            grad_out,
            pre_act,
            features,
            neigh_mean,
            w_self,
            w_neigh,
            edge_from.reshape(-1, LANES),
            edge_to.reshape(-1, LANES),
            mirror_master.reshape(-1, LANES),
            degrees.reshape(-1, LANES),
        )
        return pl.pallas_call(
            settle_kernel,
            out_shape=(jax.ShapeDtypeStruct((masters, width), BF16), weight, weight),
            in_specs=[vmem] * 2,
            out_specs=(vmem,) * 3,
        )(*[pltpu.with_memory_space_constraint(x, pltpu.VMEM) for x in sent])
    input_grad, weights = pl.pallas_call(
        functools.partial(layer_kernel, parts, block),
        out_shape=(
            jax.ShapeDtypeStruct((masters, width), BF16),
            jax.ShapeDtypeStruct((low, owners, chunk, full), BF16),
        ),
        in_specs=[pl.BlockSpec(memory_space=pltpu.SMEM)] + [vmem] * 2 + [anywhere] * 4 + [vmem] * 4,
        out_specs=(vmem, vmem),
        scratch_shapes=[
            pltpu.VMEM(features.shape, BF16),
            pltpu.VMEM(features.shape, BF16),
            pltpu.VMEM(w_self.shape, BF16),
            pltpu.VMEM(w_self.shape, BF16),
            pltpu.VMEM((2, masters, width), BF16),
            pltpu.VMEM((edges // LANES, LANES), jnp.int32),
            pltpu.VMEM((masters, width), BF16),
            pltpu.VMEM((parts, 1, slots), jnp.int32),
            pltpu.VMEM((mirror_count, width), BF16),
            pltpu.VMEM((mirror_count, width), BF16),
            pltpu.VMEM((edges, width), BF16),
            pltpu.VMEM((masters, width), F32),
            pltpu.VMEM((mirror_count, width), F32),
            pltpu.VMEM((mirror_count, width), BF16),
            pltpu.VMEM((mirror_count, width), BF16),
            pltpu.VMEM((parts // batch, HUBS, batch * slots), BF16),
            pltpu.VMEM((low, low_rows, full), BF16),
            pltpu.VMEM((low, low_rows, full), BF16),
            pltpu.VMEM((owners, chunk, full), BF16),
            pltpu.VMEM((parts // low, chunk, full), BF16),
            pltpu.VMEM((owners, chunk, full), BF16),
            pltpu.VMEM((low, owners, chunk, full), BF16),
            pltpu.SemaphoreType.DMA((4,)),
            pltpu.SemaphoreType.DMA((2,)),
            pltpu.SemaphoreType.DMA((7, parts)),
            pltpu.SemaphoreType.DMA((7, parts)),
        ],
        compiler_params=pltpu.CompilerParams(
            collective_id=0, has_side_effects=True, vmem_limit_bytes=60 * 2**20
        ),
    )(
        edge_count,
        grad_out,
        pre_act,
        features,
        neigh_mean,
        w_self,
        w_neigh,
        edge_from.reshape(-1, LANES),
        edge_to.reshape(-1, LANES),
        mirror_master.reshape(parts, 1, slots),
        degrees.reshape(-1, LANES),
    )
    weights = weights.reshape(2, w_self.shape[0], full).astype(F32)
    return (input_grad, weights[0], weights[1])


def solution(mesh):
    placed = (
        P("dom", "feat"),
        P("dom", "feat"),
        P("dom", "feat"),
        P("dom", "feat"),
        P("feat", None),
        P("feat", None),
        P("dom"),
        P("dom"),
        P("dom"),
        P("dom"),
        P("dom"),
    )
    return jax.shard_map(
        on_device,
        mesh=mesh,
        in_specs=placed,
        out_specs=(P("dom", "feat"), P("feat", None), P("feat", None)),
        check_vma=False,
    )
```

```python
import functools

import jax
import jax.numpy as jnp
from jax import lax
from jax.experimental import pallas as pl
from jax.experimental.pallas import tpu as pltpu
from jax.sharding import PartitionSpec as P

LANES = 128
HUBS = 64
MESH = pl.DeviceIdType.MESH
F32, BF16, F8 = jnp.float32, jnp.bfloat16, jnp.float8_e4m3fn


def dot(a, b, over):
    return lax.dot_general(a, b, ((over[:1], over[1:]), ((), ())), preferred_element_type=F32)


def columns_of(row):
    return jnp.transpose(jnp.broadcast_to(row, (LANES, LANES)))


def pick_rows(sinks, first, count):
    one, zero = jnp.ones((), BF16), jnp.zeros((), BF16)
    lane = lax.broadcasted_iota(jnp.int32, (LANES, LANES), 1)
    tiles = []
    for g in range(sinks.shape[0]):
        column = columns_of(sinks[g : g + 1, :])
        tiles.append(
            jnp.concatenate(
                [jnp.where(column == lane + (first + j), one, zero) for j in range(0, count, LANES)],
                axis=1,
            )
        )
    return jnp.concatenate(tiles, axis=0)


def put_rows(sources, first, count):
    one, zero = jnp.ones((), BF16), jnp.zeros((), BF16)
    row = lax.broadcasted_iota(jnp.int32, (count, LANES), 0) + first
    return jnp.concatenate(
        [jnp.where(row == sources[g : g + 1, :], one, zero) for g in range(sources.shape[0])],
        axis=1,
    )


def layer_kernel(
    parts,
    block,
    limit_ref,
    grad_ref,
    pre_ref,
    features_hbm,
    mean_hbm,
    w_self_hbm,
    w_neigh_hbm,
    source_ref,
    sink_ref,
    wanted_ref,
    degree_ref,
    out_ref,
    weights_ref,
    features_ref,
    mean_ref,
    w_self_ref,
    w_neigh_ref,
    cols,
    live,
    table,
    asked,
    replies,
    mirrors,
    picked,
    master_sum,
    mirror_sum,
    returns,
    returned,
    hits,
    partial,
    arrived,
    column_sum,
    column_arrived,
    column_total,
    full,
    load_sems,
    feat_sems,
    send_sems,
    recv_sems,
):
    me, half = lax.axis_index("dom"), lax.axis_index("feat")
    partner = 1 - half
    masters, width = grad_ref.shape
    slots = wanted_ref.shape[2]
    low, low_rows = partial.shape[0], partial.shape[1]
    owners, chunk = column_sum.shape[0], column_sum.shape[1]
    high = parts // low
    at_high, at_low = me // low, lax.rem(me, low)
    groups = block // LANES
    blocks = sink_ref.shape[0] // groups

    def peer(k):
        return lax.rem(me + k, parts)

    def giver(k):
        return lax.rem(me + (parts - k), parts)

    def rows_of(q):
        return pl.ds(pl.multiple_of(q * slots, slots), slots)

    def copy(stage, k, src, dst, device=None):
        return pltpu.make_async_remote_copy(
            src_ref=src,
            dst_ref=dst,
            send_sem=send_sems.at[stage, k],
            recv_sem=recv_sems.at[stage, k],
            device_id={"dom": peer(k) if device is None else device},
            device_id_type=MESH,
        )

    def each_peer(act, count=parts):
        lax.fori_loop(1, count, lambda k, c: (act(k), c)[1], 0)

    loads = [
        pltpu.make_async_copy(src, dst, load_sems.at[i])
        for i, (src, dst) in enumerate(
            (
                (w_neigh_hbm, w_neigh_ref),
                (features_hbm, features_ref),
                (mean_hbm, mean_ref),
                (w_self_hbm, w_self_ref),
            )
        )
    ]

    barrier = pltpu.get_barrier_semaphore()
    pl.semaphore_signal(barrier, inc=1, device_id={"feat": partner}, device_id_type=MESH)
    each_peer(
        lambda k: pl.semaphore_signal(
            barrier, inc=1, device_id={"dom": peer(k)}, device_id_type=MESH
        )
    )
    for load in loads:
        load.start()
    keep = (pre_ref[...] > 0).astype(F32)
    cols[half] = (grad_ref[...].astype(F32) * keep).astype(BF16)
    place = (
        lax.broadcasted_iota(jnp.int32, source_ref.shape, 0) * LANES
        + lax.broadcasted_iota(jnp.int32, source_ref.shape, 1)
    )
    live[...] = jnp.where(place < limit_ref[0], source_ref[...], -1)
    asked[me] = wanted_ref[me]
    pl.semaphore_wait(barrier, parts)

    exchange = pltpu.make_async_remote_copy(
        src_ref=cols.at[half],
        dst_ref=cols.at[half],
        send_sem=feat_sems.at[0],
        recv_sem=feat_sems.at[1],
        device_id={"feat": partner},
        device_id_type=MESH,
    )
    exchange.start()

    def request(k):
        return copy(0, k, wanted_ref.at[peer(k)], asked.at[me])

    each_peer(lambda k: request(k).start())
    def half_at(h):
        return pl.ds(pl.multiple_of(h * width, width), width)

    loads[0].wait()
    own = dot(cols[half], w_neigh_ref[:, half_at(half)], (1, 1))
    pltpu.make_async_remote_copy(
        src_ref=cols.at[half],
        dst_ref=cols.at[partner],
        send_sem=feat_sems.at[0],
        recv_sem=feat_sems.at[1],
        device_id={"feat": partner},
        device_id_type=MESH,
    ).wait_recv()

    both = jnp.concatenate([cols[0], cols[1]], axis=1)
    per_weight = low // 2
    for i, operand in enumerate((features_ref, mean_ref)):
        loads[1 + i].wait()
        part = dot(operand[...], both, (0, 0)).astype(BF16)
        for c in range(per_weight):
            partial[i * per_weight + c] = part[c * low_rows : (c + 1) * low_rows, :]

    def low_peer(k):
        return lax.rem(at_low + k, low)

    def low_giver(k):
        return lax.rem(at_low + (low - k), low)

    def high_peer(k):
        return lax.rem(at_high + k, high)

    def high_giver(k):
        return lax.rem(at_high + (high - k), high)

    def to_low(stage, k, src, dst):
        return copy(stage, k, src, dst, at_high * low + low_peer(k))

    def to_high(stage, k, src, dst):
        return copy(stage, k, src, dst, high_peer(k) * low + at_low)

    def guarded(act, owner):
        if owners == high:
            return act
        return lambda k: pl.when(owner(k) < owners)(lambda: act(k))

    def if_owner(act):
        if owners == high:
            act()
        else:
            pl.when(at_high < owners)(act)

    def scatter(k):
        return to_low(2, k, partial.at[low_peer(k)], arrived.at[at_low])

    each_peer(lambda k: scatter(k).start(), low)
    neigh = own + dot(cols[partner], w_neigh_ref[:, half_at(partner)], (1, 1))
    for g in range(masters // LANES):
        at = slice(g * LANES, (g + 1) * LANES)
        degree = columns_of(degree_ref[g : g + 1, :]).astype(F32)
        degree = jnp.concatenate([degree] * (width // LANES), axis=1)
        table[at, :] = (neigh[at, :] / degree).astype(BF16)

    each_peer(lambda k: copy(0, k, wanted_ref.at[peer(k)], asked.at[giver(k)]).wait_recv())

    batch = 8 if parts % 8 == 0 else 1
    hub = lax.broadcasted_iota(jnp.int32, (HUBS, slots), 0)

    def batch_at(i):
        return pl.ds(pl.multiple_of(i * batch * slots, batch * slots), batch * slots)

    def answer(i, c):
        hit = jnp.concatenate(
            [
                jnp.where(hub == asked[i * batch + j], jnp.ones((), BF16), jnp.zeros((), BF16))
                for j in range(batch)
            ],
            axis=1,
        )
        hits[i] = hit
        replies[batch_at(i), :] = dot(hit, table[:HUBS, :], (0, 0)).astype(BF16)
        return c

    lax.fori_loop(0, parts // batch, answer, 0)
    mirrors[rows_of(me), :] = replies[rows_of(me), :]

    def reply(k):
        return copy(1, k, replies.at[rows_of(peer(k)), :], mirrors.at[rows_of(me), :])

    each_peer(lambda k: reply(k).start())

    def block_at(b):
        return pl.ds(pl.multiple_of(b * groups, groups), groups)

    def edges_at(b):
        return pl.ds(pl.multiple_of(b * block, block), block)

    def from_masters(b, c):
        pick = pick_rows(sink_ref[block_at(b), :], 0, masters)
        picked[edges_at(b), :] = dot(pick, table[...], (1, 0)).astype(BF16)
        return c

    lax.fori_loop(0, blocks, from_masters, 0)

    each_peer(
        lambda k: to_low(2, k, partial.at[low_peer(k)], arrived.at[low_giver(k)]).wait_recv(), low
    )
    total = lax.fori_loop(
        1,
        low,
        lambda k, t: t + arrived[low_giver(k)].astype(F32),
        partial[at_low].astype(F32),
    ).astype(BF16)
    for c in range(owners):
        column_sum[c] = total[c * chunk : (c + 1) * chunk, :]

    def column_place():
        return lax.rem(at_high, owners)

    def scatter_high(k):
        return to_high(
            4, k, column_sum.at[lax.rem(high_peer(k), owners)], column_arrived.at[at_high]
        )

    each_peer(guarded(lambda k: scatter_high(k).start(), high_peer), high)

    each_peer(
        lambda k: copy(
            1, k, replies.at[rows_of(peer(k)), :], mirrors.at[rows_of(giver(k)), :]
        ).wait_recv()
    )
    mirror_sum[...] = jnp.zeros_like(mirror_sum)
    mirror_count = mirrors.shape[0]

    def from_mirrors(b, c):
        pick = pick_rows(sink_ref[block_at(b), :], masters, mirror_count)
        more = dot(pick, mirrors[...], (1, 0)).astype(BF16)
        row = picked[edges_at(b), :] + more
        picked[edges_at(b), :] = row
        return c

    lax.fori_loop(0, blocks, from_mirrors, 0)

    def column_spread(k):
        return to_high(5, k, column_total.at[column_place()], column_total.at[column_place()])

    def reduce_column():
        each_peer(
            lambda k: to_high(
                4,
                k,
                column_sum.at[lax.rem(high_peer(k), owners)],
                column_arrived.at[high_giver(k)],
            ).wait_recv(),
            high,
        )
        column_total[column_place()] = lax.fori_loop(
            1,
            high,
            lambda k, t: t + column_arrived[high_giver(k)].astype(F32),
            column_sum[column_place()].astype(F32),
        ).astype(BF16)
        each_peer(lambda k: column_spread(k).start(), high)

    if_owner(reduce_column)

    def to_mirrors(b, c):
        put = put_rows(live[block_at(b), :], masters, mirror_count)
        mirror_sum[...] += dot(put, picked[edges_at(b), :], (1, 0))
        return c

    lax.fori_loop(0, blocks, to_mirrors, 0)
    returns[...] = mirror_sum[...].astype(BF16)
    returned[rows_of(me), :] = returns[rows_of(me), :]

    def give_back(k):
        return copy(3, k, returns.at[rows_of(peer(k)), :], returned.at[rows_of(me), :])

    each_peer(lambda k: give_back(k).start())

    each_peer(
        guarded(
            lambda k: to_high(
                5,
                k,
                column_total.at[column_place()],
                column_total.at[lax.rem(high_giver(k), owners)],
            ).wait_recv(),
            high_giver,
        ),
        high,
    )
    full[at_low] = column_total[...]

    def spread(k):
        return to_low(6, k, column_total, full.at[at_low])

    each_peer(lambda k: spread(k).start(), low)

    loads[3].wait()
    master_sum[...] = dot(cols[0], w_self_ref[:, :width], (1, 1)) + dot(
        cols[1], w_self_ref[:, width:], (1, 1)
    )

    def to_masters(b, c):
        put = put_rows(live[block_at(b), :], 0, masters)
        master_sum[...] += dot(put, picked[edges_at(b), :], (1, 0))
        return c

    lax.fori_loop(0, blocks, to_masters, 0)

    each_peer(
        lambda k: copy(
            3, k, returns.at[rows_of(peer(k)), :], returned.at[rows_of(giver(k)), :]
        ).wait_recv()
    )
    hub_sum = lax.fori_loop(
        0,
        parts // batch,
        lambda i, t: t + dot(hits[i], returned[batch_at(i), :], (1, 0)),
        master_sum[:HUBS, :],
    )
    out_ref[:HUBS, :] = hub_sum.astype(BF16)
    out_ref[HUBS:, :] = master_sum[HUBS:, :].astype(BF16)

    each_peer(lambda k: to_low(6, k, column_total, full.at[low_giver(k)]).wait_recv(), low)
    weights_ref[...] = full[...]

    exchange.wait_send()
    each_peer(lambda k: request(k).wait_send())
    each_peer(lambda k: reply(k).wait_send())
    each_peer(lambda k: give_back(k).wait_send())
    each_peer(lambda k: scatter(k).wait_send(), low)
    each_peer(guarded(lambda k: scatter_high(k).wait_send(), high_peer), high)
    if_owner(lambda: each_peer(lambda k: column_spread(k).wait_send(), high))
    each_peer(lambda k: spread(k).wait_send(), low)


def ones_at(index, count, first):
    one, zero = jnp.ones((), BF16), jnp.zeros((), BF16)
    row = (lax.broadcasted_iota(jnp.int32, (count, LANES), 0) + first).astype(jnp.int16)
    index = index.astype(jnp.int16)
    return jnp.concatenate(
        [
            jnp.where(row == index[g : g + 1, :], one, zero).astype(F8)
            for g in range(index.shape[0])
        ],
        axis=1,
    )


def count_kernel(
    parts,
    low,
    block,
    limit_ref,
    grad_hbm,
    pre_hbm,
    features_hbm,
    mean_hbm,
    w_self_hbm,
    w_neigh_hbm,
    source_hbm,
    sink_hbm,
    wanted_hbm,
    degree_hbm,
    out_ref,
    weights_ref,
    grads,
    operands,
    w_self_ref,
    w_neigh_ref,
    edges,
    asking,
    degree_ref,
    wanted,
    cols,
    table,
    asked,
    replies,
    master_sum,
    returns,
    returned,
    hits,
    sinks,
    sources,
    count_sum,
    counts,
    partial,
    arrived,
    column_sum,
    column_arrived,
    column_total,
    full,
    load_sems,
    feat_send,
    feat_recv,
    send_sems,
    recv_sems,
):
    me, half = lax.axis_index("dom"), lax.axis_index("feat")
    partner = 1 - half
    masters, width = out_ref.shape
    mirror_count = replies.shape[0]
    slots = mirror_count // parts
    mirrors = table.at[pl.ds(masters, mirror_count), :]
    rows = masters + mirror_count
    low_rows = partial.shape[2]
    high, chunk = column_sum.shape[1], column_sum.shape[2]
    at_high, at_low = me // low, lax.rem(me, low)
    groups = block // LANES
    blocks = sinks.shape[0]
    step = mirror_count // 2
    pieces = 2

    def chunk_at(i):
        return half if i == 0 else partner

    source_ref, sink_ref = edges.at[0], edges.at[1]

    def peer(k):
        return lax.rem(me + k, parts)

    def rows_of(q):
        return pl.ds(pl.multiple_of(q * slots, slots), slots)

    def half_at(h):
        return pl.ds(pl.multiple_of(h * width, width), width)

    def copy(stage, src, dst, device):
        return pltpu.make_async_remote_copy(
            src_ref=src,
            dst_ref=dst,
            send_sem=send_sems.at[stage],
            recv_sem=recv_sems.at[stage],
            device_id={"dom": device},
            device_id_type=MESH,
        )

    def all_of(stage, ref):
        return copy(stage, ref, ref, peer(1))

    def across(i, src, dst):
        return pltpu.make_async_remote_copy(
            src_ref=src,
            dst_ref=dst,
            send_sem=feat_send.at[i],
            recv_sem=feat_recv.at[i],
            device_id={"feat": partner},
            device_id_type=MESH,
        )

    def each_peer(act, count=parts):
        lax.fori_loop(1, count, lambda k, c: (act(k), c)[1], 0)

    def load(i, *pairs):
        for src, dst in pairs:
            pltpu.make_async_copy(src, dst, load_sems.at[i]).start()

    def loaded(i, ref):
        pltpu.make_async_copy(ref, ref, load_sems.at[i]).wait()

    barrier = pltpu.get_barrier_semaphore()
    pl.semaphore_signal(barrier, inc=1, device_id={"feat": partner}, device_id_type=MESH)
    each_peer(
        lambda k: pl.semaphore_signal(
            barrier, inc=1, device_id={"dom": peer(k)}, device_id_type=MESH
        )
    )
    load(0, (grad_hbm, grads.at[0]), (pre_hbm, grads.at[1]))
    load(1, (features_hbm, operands.at[0]), (mean_hbm, operands.at[1]))
    load(2, (wanted_hbm, asking))
    load(3, (source_hbm, edges.at[0]), (sink_hbm, edges.at[1]))
    load(4, (w_neigh_hbm, w_neigh_ref))
    load(5, (degree_hbm, degree_ref))
    load(6, (w_self_hbm, w_self_ref))
    loaded(0, grads)
    keep = (grads[1] > 0).astype(F32)
    cols[half] = (grads[0].astype(F32) * keep).astype(BF16)

    per_weight = low // 2

    def weigh(h):
        for i in range(2):
            part = dot(operands[i], cols[h], (0, 0)).astype(BF16)
            for c in range(per_weight):
                partial[h, i * per_weight + c] = part[c * low_rows : (c + 1) * low_rows, :]

    def low_peer(k):
        return lax.rem(at_low + k, low)

    def low_giver(k):
        return lax.rem(at_low + (low - k), low)

    def high_peer(k):
        return lax.rem(at_high + k, high)

    def high_giver(k):
        return lax.rem(at_high + (high - k), high)

    def to_low(stage, k, src, dst):
        return copy(stage, src, dst, at_high * low + low_peer(k))

    def to_high(stage, k, src, dst):
        return copy(stage, src, dst, high_peer(k) * low + at_low)

    def scatter(i, k):
        h = chunk_at(i)
        return to_low(3 + i, k, partial.at[h, low_peer(k)], arrived.at[h, at_low])

    def scatter_high(i, k):
        h = chunk_at(i)
        return to_high(3 + pieces + i, k, column_sum.at[h, high_peer(k)], column_arrived.at[h, at_high])

    def spread_high(i, k):
        h = chunk_at(i)
        return to_high(3 + 2 * pieces + i, k, column_total.at[h, at_high], column_total.at[h, at_high])

    def spread(i, k):
        h = chunk_at(i)
        return to_low(3 + 3 * pieces + i, k, column_total.at[h], full.at[h, at_low])

    def low_batch(ref, i):
        return ref.at[chunk_at(i), pl.ds(0, low - 1)]

    def high_batch(ref, i):
        return ref.at[chunk_at(i), pl.ds(0, high - 1)]

    def add_low(i):
        h = chunk_at(i)
        all_of(3 + i, low_batch(arrived, i)).wait_recv()
        total = partial[h, at_low].astype(F32)
        for k in range(1, low):
            total = total + arrived[h, low_giver(k)].astype(F32)
        total = total.astype(BF16)
        for c in range(high):
            column_sum[h, c] = total[c * chunk : (c + 1) * chunk, :]
        each_peer(lambda k: scatter_high(i, k).start(), high)

    def add_high(i):
        h = chunk_at(i)
        all_of(3 + pieces + i, high_batch(column_arrived, i)).wait_recv()
        total = column_sum[h, at_high].astype(F32)
        for k in range(1, high):
            total = total + column_arrived[h, high_giver(k)].astype(F32)
        column_total[h, at_high] = total.astype(BF16)
        each_peer(lambda k: spread_high(i, k).start(), high)

    def pass_on(i):
        h = chunk_at(i)
        all_of(3 + 2 * pieces + i, high_batch(column_total, i)).wait_recv()
        each_peer(lambda k: spread(i, k).start(), low)
        full[h, at_low] = column_total[h]

    def finish(i):
        h = chunk_at(i)
        all_of(3 + 3 * pieces + i, low_batch(full, i)).wait_recv()
        weights_ref[h] = full[h]

    loaded(1, operands)
    weigh(half)
    loaded(2, asking)
    per_row = LANES // slots
    lane = lax.broadcasted_iota(jnp.int32, (1, LANES), 1) // slots == lax.rem(me, per_row)
    for p in range(parts):
        at = (p % per_row) * slots
        row = asking[p // per_row : p // per_row + 1, at : at + slots]
        wanted[p] = jnp.where(lane, jnp.concatenate([row] * per_row, axis=1), -1)
    asked[me] = wanted[me]
    loaded(3, edges)
    place = (
        lax.broadcasted_iota(jnp.int32, source_ref.shape, 0) * LANES
        + lax.broadcasted_iota(jnp.int32, source_ref.shape, 1)
    )
    source_ref[...] = jnp.where(place < limit_ref[0], source_ref[...], -1)
    pl.semaphore_wait(barrier, parts)

    hub_rows, other_rows = pl.ds(0, HUBS), pl.ds(HUBS, masters - HUBS)

    def exchange(i, h):
        at = (hub_rows, other_rows)[i]
        return across(i, cols.at[half, at, :], cols.at[h, at, :])

    exchange(0, half).start()

    def request(k):
        return copy(0, wanted.at[peer(k)], asked.at[me], peer(k))

    def reply(k):
        return copy(1, replies.at[rows_of(peer(k)), :], mirrors.at[rows_of(me), :], peer(k))

    def give_back(k):
        return copy(2, returns.at[rows_of(peer(k)), :], returned.at[rows_of(me), :], peer(k))

    others = pl.ds(0, (parts - 1) * slots)
    each_peer(lambda k: request(k).start())
    exchange(1, half).start()
    each_peer(lambda k: scatter(0, k).start(), low)
    loaded(4, w_neigh_ref)
    loaded(5, degree_ref)

    def scale(first, count):
        at = pl.ds(first, count)
        neigh = dot(cols[0, at, :], w_neigh_ref[:, :width], (1, 1)) + dot(
            cols[1, at, :], w_neigh_ref[:, width:], (1, 1)
        )
        for g in range(0, count, LANES):
            size = min(LANES, count - g)
            row = (first + g) // LANES
            degree = columns_of(degree_ref[row : row + 1, :])[:size, :].astype(F32)
            degree = jnp.concatenate([degree] * (width // LANES), axis=1)
            table[first + g : first + g + size, :] = (neigh[g : g + size, :] / degree).astype(BF16)

    def count_at(r, h):
        first = masters + h * step if r == 0 else h * (masters // 2) + (r - 1) * step
        return pl.ds(pl.multiple_of(first, step), step)

    def block_at(b):
        return pl.ds(b * groups, groups)

    def count(unit):
        r, c, b = unit // (2 * blocks), unit // blocks % 2, unit % blocks
        at = slice(c * (rows // 2), (c + 1) * (rows // 2))
        if r == 0:
            sinks[b, at, :] = ones_at(sink_ref[block_at(b), :], rows // 2, c * (rows // 2))
        if c == 0:
            first = masters + half * step if r == 0 else half * (masters // 2) + (r - 1) * step
            sources[b] = ones_at(source_ref[block_at(b), :], step, first)
        term = dot(sources[b], sinks[b, at, :], (1, 1))
        if b > 0:
            term = count_sum[...] + term
        if b < blocks - 1:
            count_sum[...] = term
            return
        counts[c, count_at(r, half), :] = term.astype(BF16)
        send_counts(r, c).start()

    def send_counts(r, c):
        mine = counts.at[c, count_at(r, half), :]
        return across(2 + 2 * r + c, mine, mine)

    count(0)
    count(1)
    exchange(0, partner).wait_recv()
    exchange(1, partner).wait_recv()
    weigh(partner)
    each_peer(lambda k: scatter(1, k).start(), low)
    scale(0, masters)
    all_of(0, asked.at[pl.ds(0, parts - 1)]).wait_recv()
    hub = lax.broadcasted_iota(jnp.int32, (HUBS, LANES), 0)
    for g in range(parts // per_row):
        row = asked[g * per_row]
        for p in range(1, per_row):
            row = jnp.maximum(row, asked[g * per_row + p])
        hits[:, g * LANES : (g + 1) * LANES] = jnp.where(
            hub == row, jnp.ones((), BF16), jnp.zeros((), BF16)
        )
    replies[...] = dot(hits[...], table[:HUBS, :], (0, 0)).astype(BF16)
    each_peer(lambda k: reply(k).start())
    mirrors[rows_of(me), :] = replies[rows_of(me), :]
    def count_arrives(r):
        for c in range(2):
            other = counts.at[c, count_at(r, partner), :]
            across(2 + 2 * r + c, other, other).wait_recv()

    def return_mirrors():
        count_arrives(0)
        cut = rows // 2
        own_part = dot(counts[0, masters:, :], table[:cut, :], (1, 0)) + dot(
            counts[1, masters:, : masters - cut], table[cut:masters, :], (1, 0)
        )
        all_of(1, mirrors.at[others, :]).wait_recv()
        mirror_sum = own_part + dot(
            counts[1, masters:, masters - cut :], table[masters:, :], (1, 0)
        )
        returns[...] = mirror_sum.astype(BF16)
        each_peer(lambda k: give_back(k).start())
        returned[rows_of(me), :] = returns[rows_of(me), :]

    last = masters // mirror_count
    acts = {"ret": return_mirrors}
    for i in range(pieces):
        acts["al", i] = functools.partial(add_low, i)
        acts["ah", i] = functools.partial(add_high, i)
        acts["po", i] = functools.partial(pass_on, i)
    plan = {
        "early": (),
        0: (),
        1: (),
        2: (("al", 0),),
        3: (),
        4: (),
        5: (("al", 1),),
        6: (),
        7: (("ah", 0),),
        8: (("ah", 1), "ret",),
        9: (("po", 0),),
        10: (("po", 1),),
        11: (),
        "mid": (),
        "late": (),
    }
    for a in plan["early"]:
        acts[a]()
    for unit in range(2, 2 * (last + 1) * blocks):
        count(unit)
        for a in plan.get(unit, ()):
            acts[a]()
    loaded(6, w_self_ref)

    def settle(h):
        at = pl.ds(pl.multiple_of(h * (masters // 2), masters // 2), masters // 2)
        total = (
            dot(cols[0, at, :], w_self_ref[:, :width], (1, 1))
            + dot(cols[1, at, :], w_self_ref[:, width:], (1, 1))
            + dot(counts[0, at, :], table[: rows // 2, :], (1, 0))
            + dot(counts[1, at, :], table[rows // 2 :, :], (1, 0))
        )
        master_sum[at, :] = total
        out_ref[at, :] = total.astype(BF16)

    settle(half)
    for a in plan["mid"]:
        acts[a]()
    for r in range(1, last + 1):
        count_arrives(r)
    settle(partner)
    for a in plan["late"]:
        acts[a]()
    all_of(2, returned.at[others, :]).wait_recv()
    hub_sum = master_sum[:HUBS, :] + dot(hits[...], returned[...], (1, 0))
    out_ref[:HUBS, :] = hub_sum.astype(BF16)
    for i in range(pieces):
        finish(i)

    exchange(0, half).wait_send()
    exchange(1, half).wait_send()
    for r in range(last + 1):
        for c in range(2):
            send_counts(r, c).wait_send()
    all_of(0, wanted.at[pl.ds(0, parts - 1)]).wait_send()
    all_of(1, replies.at[others, :]).wait_send()
    all_of(2, returns.at[others, :]).wait_send()
    for i in range(pieces):
        all_of(3 + i, low_batch(partial, i)).wait_send()
        all_of(3 + pieces + i, high_batch(column_sum, i)).wait_send()
        all_of(3 + 2 * pieces + i, high_batch(column_total, i)).wait_send()
        all_of(3 + 3 * pieces + i, low_batch(full, i)).wait_send()


def settle_kernel(grad_ref, weights_ref, out_ref, self_ref, neigh_ref):
    out_ref[...] = grad_ref[...]
    halves, low, high, chunk, width = weights_ref.shape
    rows = (low // 2) * high * chunk
    for w, ref in enumerate((self_ref, neigh_ref)):
        for h in range(halves):
            block = weights_ref[h, w * (low // 2) : (w + 1) * (low // 2)].reshape(rows, width)
            ref[:, h * width : (h + 1) * width] = block.astype(F32)


def on_device(
    features,
    grad_out,
    pre_act,
    neigh_mean,
    w_self,
    w_neigh,
    edge_from,
    edge_to,
    edge_count,
    mirror_master,
    degrees,
):
    masters, width = features.shape
    parts = lax.axis_size("dom")
    mirror_count = mirror_master.shape[0]
    slots = mirror_count // parts
    edges = edge_from.shape[0]
    full = w_self.shape[1]
    weight_rows = 2 * w_self.shape[0]
    low = 2
    while parts % (4 * low) == 0 and 4 * low * low <= parts:
        low *= 2
    low_rows = weight_rows // low
    owners = min(parts // low, low_rows // 16)
    chunk = low_rows // owners
    batch = 8 if parts % 8 == 0 else 1
    block = min(edges, 2048 if masters + mirror_count <= 2048 else 256)
    vmem = pl.BlockSpec(memory_space=pltpu.VMEM)
    anywhere = pl.BlockSpec(memory_space=pl.ANY)
    step = mirror_count // 2
    if (
        masters + mirror_count <= 2048
        and owners * low == parts
        and parts % (LANES // slots) == 0
        and masters % mirror_count == 0
        and edges % 4096 == 0
        and chunk % 16 == 0
    ):
        high = owners
        part = chunk
        count_block = edges // 2
        weight = jax.ShapeDtypeStruct(w_self.shape, F32)
        rows = masters + mirror_count
        sent = pl.pallas_call(
            functools.partial(count_kernel, parts, low, count_block),
            out_shape=(
                pltpu.VMEM((masters, width), BF16),
                pltpu.VMEM((2, low, high, part, width), BF16),
            ),
            in_specs=[pl.BlockSpec(memory_space=pltpu.SMEM)] + [anywhere] * 10,
            out_specs=(vmem, vmem),
            scratch_shapes=[
                pltpu.VMEM((2, masters, width), BF16),
                pltpu.VMEM((2, masters, width), BF16),
                pltpu.VMEM(w_self.shape, BF16),
                pltpu.VMEM(w_self.shape, BF16),
                pltpu.VMEM((2, edges // LANES, LANES), jnp.int32),
                pltpu.VMEM((mirror_count // LANES, LANES), jnp.int32),
                pltpu.VMEM((masters // LANES, LANES), jnp.int32),
                pltpu.VMEM((parts, 1, LANES), jnp.int32),
                pltpu.VMEM((2, masters, width), BF16),
                pltpu.VMEM((rows, width), BF16),
                pltpu.VMEM((parts, 1, LANES), jnp.int32),
                pltpu.VMEM((mirror_count, width), BF16),
                pltpu.VMEM((masters, width), F32),
                pltpu.VMEM((mirror_count, width), BF16),
                pltpu.VMEM((mirror_count, width), BF16),
                pltpu.VMEM((HUBS, mirror_count), BF16),
                pltpu.VMEM((edges // count_block, rows, count_block), F8),
                pltpu.VMEM((edges // count_block, step, count_block), F8),
                pltpu.VMEM((step, rows // 2), F32),
                pltpu.VMEM((2, rows, rows // 2), BF16),
                pltpu.VMEM((2, low, high * part, width), BF16),
                pltpu.VMEM((2, low, high * part, width), BF16),
                pltpu.VMEM((2, high, part, width), BF16),
                pltpu.VMEM((2, high, part, width), BF16),
                pltpu.VMEM((2, high, part, width), BF16),
                pltpu.VMEM((2, low, high, part, width), BF16),
                pltpu.SemaphoreType.DMA((7,)),
                pltpu.SemaphoreType.DMA((4 + 2 * (masters // mirror_count),)),
                pltpu.SemaphoreType.DMA((4 + 2 * (masters // mirror_count),)),
                pltpu.SemaphoreType.DMA((11,)),
                pltpu.SemaphoreType.DMA((11,)),
            ],
            compiler_params=pltpu.CompilerParams(
                collective_id=1, has_side_effects=True, vmem_limit_bytes=54 * 2**20
            ),
        )(
            edge_count,
            grad_out,
            pre_act,
            features,
            neigh_mean,
            w_self,
            w_neigh,
            edge_from.reshape(-1, LANES),
            edge_to.reshape(-1, LANES),
            mirror_master.reshape(-1, LANES),
            degrees.reshape(-1, LANES),
        )
        return pl.pallas_call(
            settle_kernel,
            out_shape=(jax.ShapeDtypeStruct((masters, width), BF16), weight, weight),
            in_specs=[vmem] * 2,
            out_specs=(vmem,) * 3,
        )(*[pltpu.with_memory_space_constraint(x, pltpu.VMEM) for x in sent])
    input_grad, weights = pl.pallas_call(
        functools.partial(layer_kernel, parts, block),
        out_shape=(
            jax.ShapeDtypeStruct((masters, width), BF16),
            jax.ShapeDtypeStruct((low, owners, chunk, full), BF16),
        ),
        in_specs=[pl.BlockSpec(memory_space=pltpu.SMEM)] + [vmem] * 2 + [anywhere] * 4 + [vmem] * 4,
        out_specs=(vmem, vmem),
        scratch_shapes=[
            pltpu.VMEM(features.shape, BF16),
            pltpu.VMEM(features.shape, BF16),
            pltpu.VMEM(w_self.shape, BF16),
            pltpu.VMEM(w_self.shape, BF16),
            pltpu.VMEM((2, masters, width), BF16),
            pltpu.VMEM((edges // LANES, LANES), jnp.int32),
            pltpu.VMEM((masters, width), BF16),
            pltpu.VMEM((parts, 1, slots), jnp.int32),
            pltpu.VMEM((mirror_count, width), BF16),
            pltpu.VMEM((mirror_count, width), BF16),
            pltpu.VMEM((edges, width), BF16),
            pltpu.VMEM((masters, width), F32),
            pltpu.VMEM((mirror_count, width), F32),
            pltpu.VMEM((mirror_count, width), BF16),
            pltpu.VMEM((mirror_count, width), BF16),
            pltpu.VMEM((parts // batch, HUBS, batch * slots), BF16),
            pltpu.VMEM((low, low_rows, full), BF16),
            pltpu.VMEM((low, low_rows, full), BF16),
            pltpu.VMEM((owners, chunk, full), BF16),
            pltpu.VMEM((parts // low, chunk, full), BF16),
            pltpu.VMEM((owners, chunk, full), BF16),
            pltpu.VMEM((low, owners, chunk, full), BF16),
            pltpu.SemaphoreType.DMA((4,)),
            pltpu.SemaphoreType.DMA((2,)),
            pltpu.SemaphoreType.DMA((7, parts)),
            pltpu.SemaphoreType.DMA((7, parts)),
        ],
        compiler_params=pltpu.CompilerParams(
            collective_id=0, has_side_effects=True, vmem_limit_bytes=60 * 2**20
        ),
    )(
        edge_count,
        grad_out,
        pre_act,
        features,
        neigh_mean,
        w_self,
        w_neigh,
        edge_from.reshape(-1, LANES),
        edge_to.reshape(-1, LANES),
        mirror_master.reshape(parts, 1, slots),
        degrees.reshape(-1, LANES),
    )
    weights = weights.reshape(2, w_self.shape[0], full).astype(F32)
    return (input_grad, weights[0], weights[1])


def solution(mesh):
    placed = (
        P("dom", "feat"),
        P("dom", "feat"),
        P("dom", "feat"),
        P("dom", "feat"),
        P("feat", None),
        P("feat", None),
        P("dom"),
        P("dom"),
        P("dom"),
        P("dom"),
        P("dom"),
    )
    return jax.shard_map(
        on_device,
        mesh=mesh,
        in_specs=placed,
        out_specs=(P("dom", "feat"), P("feat", None), P("feat", None)),
        check_vma=False,
    )
```
